256 devices in a mesh: dom: 64 (over z_hi, x, y, core), slab: 4 (over z_lo).
Axes of the slice: x: 4, y: 4, z: 8 (z_hi: 2, z_lo: 4; z = z_hi * 4 + z_lo), core: 2. Of those that a mesh axis runs over, the one named last changes fastest.
Arguments:
- features: bfloat16 [32768, 128], P(('dom', 'slab')), may hold values from -6 to 6
- cotangent: bfloat16 [32768, 128], P(('dom', 'slab')), may hold values from -6 to 6
- positions: float32 [3, 32768], P(None, ('dom', 'slab')), may hold values from 0 to 1, as said below
- neighbours: int32 [16, 32768], P(None, ('dom', 'slab')), may hold values from 0 to 191
- counts: int32 [32768], P(('dom', 'slab')), may hold values from 4 to 16, as said below
- k_index: int32 [3, 2048], replicated, may hold values from -8 to 8, as said below
- k_filter: float32 [2048, 128], replicated, may hold values from -0.125 to 0.125
- w_radial: bfloat16 [16, 128], replicated, may hold values from -1.5 to 1.5
- w_out: bfloat16 [128, 128], replicated, may hold values from -0.5 to 0.5
Outputs:
- d_features: float32 [32768, 128], P(('dom', 'slab'))
- d_positions: float32 [3, 32768], P(None, ('dom', 'slab'))
- d_filter: float32 [2048, 128], P(('dom', 'slab'))
- d_radial: float32 [16, 128], replicated
- d_out: float32 [128, 128], replicated
The draws below stay inside these ranges and needn't reach their ends.
Inputs may be any that keep to these rules, and one draw needn't show every extreme that they name: Atoms of domain (a, b) have positions[0] in [a / 64, (a + 1) / 64) and positions[1] in [b / 4, (b + 1) / 4). `neighbours`: entries index the domain's ghost buffer: its own 128 atoms, then 4 groups of 16 ghost atoms as the steps define. Slot s of atom i is live when s < counts[i]; the first atom of every domain uses all 16 slots. `k_index`: the 2048 vectors (columns) are distinct and non-zero, and no vector's negative is among them.
All inputs are finite; a program needn't handle non-finite values.
Results may differ from the reference program's by a relative error of at most 0.0054.
Values may be sent and summed in bfloat16 or wider, within the bound.
A program may use at most 64 MiB of HBM per device.

```python
import math
import jax
import jax.numpy as jnp
from jax import lax

A_DEV = 128
NB = 16
C = 128
K = 2048
H = 128
R = 16
GH = 16
ATOMS = 32768
N_DOM = 64
N_SLAB = 4


def draw_positions(key, part):
    uniform_draw = jax.random.uniform(key, (3, ATOMS), jnp.float32)
    blocks = jnp.arange(ATOMS, dtype=jnp.int32) // A_DEV
    first_cell = (blocks // N_SLAB).astype(jnp.float32)
    second_cell = (blocks % N_SLAB).astype(jnp.float32)
    return jnp.stack([(first_cell + uniform_draw[0]) / N_DOM, (second_cell + uniform_draw[1]) / N_SLAB, uniform_draw[2]])


def draw_counts(key, part):
    drawn = jax.random.randint(key, (ATOMS,), NB // 4, NB + 1)
    leading = jnp.arange(ATOMS, dtype=jnp.int32) % A_DEV == 0
    return jnp.where(leading, NB, drawn).astype(jnp.int32)


def draw_k_index(key, part):
    side_len = 17
    cube_cells = side_len * side_len * side_len
    shuffled = jax.random.permutation(jax.random.fold_in(key, 7), jnp.arange(cube_cells, dtype=jnp.int32))
    first_idx = shuffled // (side_len * side_len) - 8
    second_idx = shuffled // side_len % side_len - 8
    third_idx = shuffled % side_len - 8
    upper_half = (first_idx > 0) | (first_idx == 0) & (second_idx > 0) | (first_idx == 0) & (second_idx == 0) & (third_idx > 0)
    ranking = jnp.argsort(jnp.where(upper_half, 0, 1).astype(jnp.int32), stable=True)
    chosen = ranking[:K]
    return jnp.stack([first_idx[chosen], second_idx[chosen], third_idx[chosen]]).astype(jnp.int32)


def with_ends(array, key, least, high):
    longest = array.shape.index(max(array.shape))
    spots = []
    for shift in (0, 1):
        where = [jax.random.randint(jax.random.fold_in(key, axis), (), 0, length) for axis, length in enumerate(array.shape)]
        where[longest] = (where[longest] + shift) % array.shape[longest]
        spots.append(tuple(where))
    return array.at[spots[0]].set(least).at[spots[1]].set(high)


def steps_of(rng, extent, pieces, smallest, largest):
    loudness = 1.0
    for axis_at, shards_of in pieces:
        draws = jax.random.uniform(jax.random.fold_in(jax.random.fold_in(rng, 6), axis_at), (shards_of,), jnp.float32, smallest / len(pieces), largest / len(pieces))
        loudness = loudness * jnp.repeat(jnp.exp(draws), extent[axis_at] // shards_of).reshape((-1,) + (1,) * (len(extent) - 1 - axis_at))
    return loudness


def bell_draw(stream_key, shape, width, reach, cuts=(), kind=jnp.bfloat16):
    values = width * jax.random.normal(stream_key, shape, jnp.float32)
    if cuts:
        values = values * steps_of(stream_key, shape, cuts, -0.22, 0.18)
    return jnp.clip(values, -reach, reach).astype(kind)


def setup_inputs(seed: int = 0) -> dict:
    seeds = jax.random.split(jax.random.key(seed), 10)
    return {
        "features": bell_draw(seeds[0], (ATOMS, C), 1.0, 6.0, ((0, 256),)),
        "cotangent": bell_draw(seeds[1], (ATOMS, C), 1.0, 6.0, ((0, 256),)),
        "positions": draw_positions(jax.random.fold_in(seeds[9], 71), 0),
        "neighbours": with_ends(jax.random.randint(seeds[3], (NB, ATOMS), 0, A_DEV + 4 * GH), jax.random.fold_in(seeds[3], 1), 0, (A_DEV + 4 * GH) - 1).astype(jnp.int32),
        "counts": draw_counts(jax.random.fold_in(seeds[9], 71), 0),
        "k_index": draw_k_index(jax.random.fold_in(seeds[9], 71), 0),
        "k_filter": bell_draw(seeds[6], (K, C), K ** -0.5, 0.125, (), jnp.float32),
        "w_radial": bell_draw(seeds[7], (R, H), R ** -0.5, 1.5),
        "w_out": bell_draw(seeds[8], (H, C), H ** -0.5, 0.5),
    }


TWO_PI = 2.0 * math.pi
HIGHEST = lax.Precision.HIGHEST

def phases(positions, k_vectors):
    phase_arg = TWO_PI * (positions[0][:, None] * k_vectors[0][None, :] + positions[1][:, None] * k_vectors[1][None, :] + positions[2][:, None] * k_vectors[2][None, :])
    return (jnp.cos(phase_arg), jnp.sin(phase_arg))

def contract_rows(first_op, second_op):
    return lax.dot_general(first_op, second_op, (((0,), (0,)), ((), ())), preferred_element_type=jnp.float32)

def contract_cols(first_op, second_op):
    return lax.dot_general(first_op, second_op, (((1,), (1,)), ((), ())), preferred_element_type=jnp.float32)

def structure_terms(features, cotangent, positions, k_vectors):
    cosine, sine_val = phases(positions, k_vectors)
    cos_half = cosine.astype(jnp.bfloat16)
    sin_half = sine_val.astype(jnp.bfloat16)
    return (contract_rows(cos_half, features), contract_rows(sin_half, features), contract_rows(cos_half, cotangent), contract_rows(sin_half, cotangent))

def long_backward(features, cotangent, positions, k_vectors, shares, pos_unit):
    fs_re, fs_im, fg_re, fg_im = shares
    cosine, sine_val = phases(positions, k_vectors)
    cos_half = cosine.astype(jnp.bfloat16)
    sin_half = sine_val.astype(jnp.bfloat16)
    d_feat = jnp.dot(cos_half, fg_re, preferred_element_type=jnp.float32) + jnp.dot(sin_half, fg_im, preferred_element_type=jnp.float32)
    along_re = contract_cols(cotangent, fs_re) + contract_cols(features, fg_re)
    along_im = contract_cols(cotangent, fs_im) + contract_cols(features, fg_im)
    weight = cosine * along_im - sine_val * along_re
    d_pos = pos_unit * lax.dot_general(k_vectors, weight, (((1,), (1,)), ((), ())), precision=HIGHEST, preferred_element_type=jnp.float32)
    return (d_feat, d_pos)

def radial_rates(levels):
    steps_n = jnp.arange(levels, dtype=jnp.float32)
    return 0.5 * jnp.exp(steps_n * (math.log(16.0) / (levels - 1)))

def pair_backward(buf_feat, buf_pos, own_pos, cotangent, neighbours, counts, w_radial, w_out, rates, pos_unit):
    slots, atom_count = neighbours.shape
    buffer_rows = buf_feat.shape[0]
    flat_index = neighbours.reshape(-1)
    target_pos = jnp.take(buf_pos, flat_index, axis=1)
    source_pos = jnp.tile(own_pos, (1, slots))
    offsets = target_pos - source_pos
    chord = jnp.sin(TWO_PI * offsets)
    dist2 = lax.optimization_barrier(jnp.sum(chord * chord, axis=0))
    rbf = jnp.exp(-rates[:, None] * dist2[None, :])
    rbf_half = rbf.astype(jnp.bfloat16)
    pre_act = lax.dot_general(rbf_half, w_radial, (((0,), (0,)), ((), ())), preferred_element_type=jnp.float32)
    gate_prob = jax.nn.sigmoid(pre_act)
    act_half = (pre_act * gate_prob).astype(jnp.bfloat16)
    filt_val = jnp.dot(act_half, w_out, preferred_element_type=jnp.float32)
    live_mask = (lax.broadcasted_iota(jnp.int32, (slots, atom_count), 0) < counts[None, :]).reshape(-1).astype(jnp.float32)
    cot_rep = jnp.tile(cotangent, (slots, 1)).astype(jnp.float32)
    weight_g = (live_mask / math.sqrt(slots))[:, None] * cot_rep
    d_buf_feat = jnp.zeros((buffer_rows, cotangent.shape[1]), jnp.float32).at[flat_index].add(weight_g * filt_val)
    feat_rows = jnp.take(buf_feat, flat_index, axis=0)
    dphi = (weight_g * feat_rows).astype(jnp.bfloat16)
    pair_out = contract_rows(act_half, dphi)
    d_act = contract_cols(dphi, w_out)
    dpre = (d_act * gate_prob * (1.0 + pre_act * (1.0 - gate_prob))).astype(jnp.bfloat16)
    pair_radial = lax.dot_general(rbf_half, dpre, (((1,), (0,)), ((), ())), preferred_element_type=jnp.float32)
    d_rbf = contract_cols(w_radial, dpre)
    d_chord2 = -lax.optimization_barrier(jnp.sum(d_rbf * rates[:, None] * rbf, axis=0))
    dmove = 2.0 * pos_unit * d_chord2[None, :] * chord * jnp.cos(TWO_PI * offsets)
    d_buf_pos = jnp.zeros((3, buffer_rows), jnp.float32).at[:, flat_index].add(dmove)
    d_own_pos = -lax.optimization_barrier(jnp.sum(dmove.reshape(3, slots, atom_count), axis=1))
    return (d_buf_feat, d_buf_pos, d_own_pos, pair_radial, pair_out)

def reference(features, cotangent, positions, neighbours, counts, k_index, k_filter, w_radial, w_out):
    devices = N_DOM * N_SLAB
    scale_norm = 1.0 / math.sqrt(ATOMS)
    pos_unit = 1.0 / math.sqrt(K)
    k_vectors = k_index.astype(jnp.float32)
    feat_blocks = features.reshape(devices, A_DEV, C)
    cot_blocks = cotangent.reshape(devices, A_DEV, C)
    pos_blocks = positions.reshape(3, devices, A_DEV).transpose(1, 0, 2)

    def add_terms(totals, blocks):
        partials = structure_terms(blocks[0], blocks[1], blocks[2], k_vectors)
        return (tuple((first_op + second_op for first_op, second_op in zip(totals, partials))), None)
    zeros_kc = jnp.zeros((K, C), jnp.float32)
    summed, _ = lax.scan(add_terms, (zeros_kc, zeros_kc, zeros_kc, zeros_kc), (feat_blocks, cot_blocks, pos_blocks))
    s_re, s_im, g_re, g_im = [scale_norm * value_kc for value_kc in summed]
    d_filter = s_re * g_re + s_im * g_im
    shares = tuple(((k_filter * value_kc).astype(jnp.bfloat16) for value_kc in (s_re, s_im, g_re, g_im)))

    def long_block(blocks):
        return long_backward(blocks[0], blocks[1], blocks[2], k_vectors, shares, pos_unit)
    d_long, dpos_long = lax.map(long_block, (feat_blocks, cot_blocks, pos_blocks))
    grid_feat = features.reshape(N_DOM, N_SLAB, A_DEV, C)
    grid_pos = positions.reshape(3, N_DOM, N_SLAB, A_DEV)

    def feat_face(face):
        return grid_feat[:, :, face * GH:(face + 1) * GH]

    def pos_face(face):
        return grid_pos[:, :, :, face * GH:(face + 1) * GH]
    ghost_feat = [jnp.roll(feat_face(1), 1, 0), jnp.roll(feat_face(0), -1, 0), jnp.roll(feat_face(3), 1, 1), jnp.roll(feat_face(2), -1, 1)]
    ghost_pos = [jnp.roll(pos_face(1), 1, 1), jnp.roll(pos_face(0), -1, 1), jnp.roll(pos_face(3), 1, 2), jnp.roll(pos_face(2), -1, 2)]
    buffer_rows = A_DEV + 4 * GH
    buf_feat = jnp.concatenate([grid_feat] + ghost_feat, axis=2).reshape(devices, buffer_rows, C)
    buf_pos = jnp.concatenate([grid_pos] + ghost_pos, axis=3).reshape(3, devices, buffer_rows).transpose(1, 0, 2)
    nbr_blocks = neighbours.reshape(NB, devices, A_DEV).transpose(1, 0, 2)
    count_blocks = counts.reshape(devices, A_DEV)
    rates = radial_rates(R)

    def pair_block(blocks):
        return pair_backward(blocks[0], blocks[1], blocks[2], blocks[3], blocks[4], blocks[5], w_radial, w_out, rates, pos_unit)
    d_buf_feat, d_buf_pos, d_own_pos, pair_radial, pair_out = lax.map(pair_block, (buf_feat, buf_pos, pos_blocks, cot_blocks, nbr_blocks, count_blocks))
    grid_dfeat = d_buf_feat.reshape(N_DOM, N_SLAB, buffer_rows, C)
    ghost_dfeat = [grid_dfeat[:, :, A_DEV + face * GH:A_DEV + (face + 1) * GH] for face in range(4)]
    returned = [jnp.roll(ghost_dfeat[0], -1, 0), jnp.roll(ghost_dfeat[1], 1, 0), jnp.roll(ghost_dfeat[2], -1, 1), jnp.roll(ghost_dfeat[3], 1, 1)]
    feat_return = jnp.concatenate([returned[1], returned[0], returned[3], returned[2], jnp.zeros((N_DOM, N_SLAB, A_DEV - 4 * GH, C), jnp.float32)], axis=2)
    short_feat = grid_dfeat[:, :, :A_DEV] + feat_return
    grid_dpos = d_buf_pos.transpose(1, 0, 2).reshape(3, N_DOM, N_SLAB, buffer_rows)
    ghost_dpos = [grid_dpos[:, :, :, A_DEV + face * GH:A_DEV + (face + 1) * GH] for face in range(4)]
    returned_pos = [jnp.roll(ghost_dpos[0], -1, 1), jnp.roll(ghost_dpos[1], 1, 1), jnp.roll(ghost_dpos[2], -1, 2), jnp.roll(ghost_dpos[3], 1, 2)]
    pos_return = jnp.concatenate([returned_pos[1], returned_pos[0], returned_pos[3], returned_pos[2], jnp.zeros((3, N_DOM, N_SLAB, A_DEV - 4 * GH), jnp.float32)], axis=3)
    own_moves = d_own_pos.transpose(1, 0, 2).reshape(3, N_DOM, N_SLAB, A_DEV)
    short_pos = grid_dpos[:, :, :, :A_DEV] + pos_return + own_moves
    d_features = d_long.reshape(ATOMS, C) + short_feat.reshape(ATOMS, C)
    d_positions = dpos_long.transpose(1, 0, 2).reshape(3, ATOMS) + short_pos.reshape(3, ATOMS)
    d_radial = scale_norm * lax.optimization_barrier(jnp.sum(pair_radial, axis=0))
    d_out = scale_norm * lax.optimization_barrier(jnp.sum(pair_out, axis=0))
    return (d_features, d_positions, d_filter, d_radial, d_out)
```

```python
import functools
import math

import jax
import jax.numpy as jnp
from jax import lax
from jax.experimental import pallas as pl
from jax.experimental.pallas import tpu as pltpu
from jax.sharding import PartitionSpec as P

Z_HI, N_X, N_Y, N_CORE = 2, 4, 4, 2
EDGE = 8
F32 = jnp.float32
BF16 = jnp.bfloat16

SIN_C = (3.1415926401307077, -5.167710083507896, 2.550077523214726, -0.5982912856213906, 0.07765766030763246)
COS_C = (
    0.9999999997799044,
    -4.934802137078806,
    4.058709159555702,
    -1.3352120030438075,
    0.23493731378604543,
    -0.024396324301093893,
)


def horner(coefs, u):
    y = coefs[-1] * u + coefs[-2]
    for k in coefs[-3::-1]:
        y = y * u + k
    return y


def turns(t):
    r = t - jnp.round(t)
    u = r * r
    s = r * horner(SIN_C, u)
    c = horner(COS_C, u)
    return 1.0 - 2.0 * (s * s), 2.0 * (s * c)


def split3(v):
    hi = v.astype(BF16)
    rest = v - hi.astype(F32)
    mid = rest.astype(BF16)
    lo = (rest - mid.astype(F32)).astype(BF16)
    return jnp.concatenate([hi.astype(F32), mid.astype(F32), lo.astype(F32), jnp.zeros_like(v)], axis=0).astype(BF16)


def nn(a, b):
    return lax.dot_general(a, b, (((1,), (0,)), ((), ())), preferred_element_type=F32)


def nt(a, b):
    return lax.dot_general(a, b, (((1,), (1,)), ((), ())), preferred_element_type=F32)


def body(
    n_slab,
    feat_ref,
    cot_ref,
    pos_ref,
    nbr_ref,
    cnt_ref,
    kidx_ref,
    kfil_ref,
    wrad_ref,
    wout_ref,
    o_feat,
    o_pos,
    o_filter,
    o_radial,
    o_out,
    gfc,
    gpos,
    hfeat,
    hpos,
    csf,
    csh,
    ysend,
    yown,
    yrecv,
    zsend,
    zrecv,
    wbuf,
    kf8,
    outs_f,
    outs_p,
    outr_f,
    outr_p,
    own_f,
    own_p,
    kcol,
    krow,
    bufft,
    possp,
    cott,
    wradt,
    woutt,
    dbf,
    dbp,
    dgp,
    ownp,
    pwo,
    pwr,
    retf,
    retp,
    pw_a,
    pw_ar,
    pw_b,
    pw_br,
    pw_c,
    pw_cr,
    pw_d,
    loc_sem,
    g_s,
    g_r,
    gp_s,
    gp_r,
    h_s,
    h_r,
    hp_s,
    hp_r,
    y_s,
    y_r,
    z_s,
    z_r,
    za_s,
    za_r,
    ya_s,
    ya_r,
    of_s,
    of_r,
    op_s,
    op_r,
    rf_s,
    rf_r,
    rp_s,
    rp_r,
    pa_s,
    pa_r,
    pb_s,
    pb_r,
    pc_s,
    pc_r,
    pd_s,
    pd_r,
):
    atoms, chan = feat_ref.shape
    slots = nbr_ref.shape[0]
    k_total = kidx_ref.shape[1]
    n_z = Z_HI * n_slab
    group = N_X * N_CORE
    k_loc = N_Y * n_z * EDGE
    n_dom = Z_HI * N_X * N_Y * N_CORE
    face = atoms // 8
    buf_rows = atoms + 4 * face
    nu = 1.0 / math.sqrt(atoms * n_dom * n_slab)
    mu = 1.0 / math.sqrt(k_total)

    dom = lax.axis_index("dom")
    slab = lax.axis_index("slab")
    core = lax.rem(dom, N_CORE)
    y = lax.rem(lax.div(dom, N_CORE), N_Y)
    x = lax.rem(lax.div(dom, N_CORE * N_Y), N_X)
    zh = lax.div(dom, N_CORE * N_Y * N_X)
    z = zh * n_slab + slab

    def dom_of(zh_, x_, y_, c_):
        return ((zh_ * N_X + x_) * N_Y + y_) * N_CORE + c_

    def at_xc(dx, dc):
        return (dom_of(zh, lax.rem(x + dx, N_X), y, lax.rem(core + dc, N_CORE)), slab)

    def at_y(d):
        return (dom_of(zh, x, lax.rem(y + d, N_Y), core), slab)

    def at_z(d):
        zz = lax.rem(z + d, n_z)
        return (dom_of(lax.div(zz, n_slab), x, y, core), lax.rem(zz, n_slab))

    at_dom = (
        (lax.rem(dom + n_dom - 1, n_dom), slab),
        (lax.rem(dom + 1, n_dom), slab),
        (dom, lax.rem(slab + n_slab - 1, n_slab)),
        (dom, lax.rem(slab + 1, n_slab)),
    )

    def copy(src, dst, ss, rs, dev):
        return pltpu.make_async_remote_copy(
            src_ref=src, dst_ref=dst, send_sem=ss, recv_sem=rs, device_id=dev, device_id_type=pl.DeviceIdType.MESH
        )

    xc = [(dx, dc) for dx in range(N_X) for dc in range(N_CORE)][1:]
    slot_of = {p: p[0] * N_CORE + p[1] for p in xc}
    far_first = sorted(xc, key=lambda p: -min(p[0], N_X - p[0]))
    near_first = far_first[::-1]

    peers = [at_xc(*p) for p in xc] + [at_y(d) for d in range(1, N_Y)] + [at_z(d) for d in range(1, n_z)]
    peers += [at_dom[0], at_dom[1]]
    barrier = pltpu.get_barrier_semaphore()
    for dev in peers:
        pl.semaphore_signal(barrier, inc=1, device_id=dev, device_id_type=pl.DeviceIdType.MESH)

    k_first = pl.multiple_of((dom * n_slab + slab) * EDGE, EDGE)
    load_filter = pltpu.make_async_copy(kfil_ref.at[pl.ds(k_first, EDGE)], kf8, loc_sem)
    load_filter.start()

    gfc[0, :, 0:chan] = feat_ref[...]
    gfc[0, :, chan : 2 * chan] = cot_ref[...]
    gpos[0] = jnp.zeros((8, atoms), F32)
    gpos[0, 0:3] = pos_ref[...]

    pl.semaphore_wait(barrier, len(peers))

    sent = []
    waits = {}

    def send(name, key, c):
        c.start()
        sent.append(c)
        waits[(name, key)] = c

    for p in far_first:
        s = slot_of[p]
        send("gp", s, copy(gpos.at[0], gpos.at[s], gp_s.at[s - 1], gp_r.at[s - 1], at_xc(*p)))
    for g in range(4):
        f = g ^ 1
        dev = at_dom[f]
        send("h", g, copy(feat_ref.at[pl.ds(f * face, face)], hfeat.at[g], h_s.at[g], h_r.at[g], dev))
        send("hp", g, copy(gpos.at[0], hpos.at[g], hp_s.at[g], hp_r.at[g], dev))
    for p in far_first:
        s = slot_of[p]
        send("g", s, copy(gfc.at[0], gfc.at[s], g_s.at[s - 1], g_r.at[s - 1], at_xc(*p)))

    m = lax.broadcasted_iota(jnp.int32, (k_loc, k_total), 0)
    e = jnp.bitwise_and(m, EDGE - 1)
    bz = lax.rem(lax.div(m, EDGE) + z, n_z)
    by = lax.rem(lax.div(m, EDGE * n_z) + y, N_Y)
    row = (dom_of(lax.div(bz, n_slab), x, by, core) * n_slab + lax.rem(bz, n_slab)) * EDGE + e
    pick = jnp.where(row == lax.broadcasted_iota(jnp.int32, (k_loc, k_total), 1), 1.0, 0.0).astype(BF16)
    k8 = jnp.concatenate([kidx_ref[...].astype(F32), jnp.zeros((5, k_total), F32)], axis=0)
    krow[...] = nt(k8.astype(BF16), pick)
    kcol[...] = nt(pick, jnp.concatenate([k8, k8, k8, jnp.zeros_like(k8)], axis=0).astype(BF16)).astype(BF16)

    def tables(s):
        t = nn(kcol[...], split3(gpos[s]))
        cosine, sine = turns(t)
        lanes = slice(s * atoms, (s + 1) * atoms)
        both = jnp.stack([cosine.reshape(-1, EDGE, atoms), sine.reshape(-1, EDGE, atoms)], axis=1)
        csf[:, :, lanes] = both.reshape(-1, EDGE, atoms)
        csh[:, lanes] = both.reshape(-1, atoms).astype(BF16)

    tables(0)
    for p in near_first:
        s = slot_of[p]
        waits[("gp", s)].wait_recv()
        tables(s)
    for p in near_first:
        waits[("g", slot_of[p])].wait_recv()

    fc_all = gfc[...].reshape(group * atoms, 2 * chan)
    y_rows = n_z * 2 * EDGE
    y_order = sorted(range(1, N_Y), key=lambda d: -min(d, N_Y - d))
    for d in y_order + [0]:
        part = nn(csh[d * y_rows : (d + 1) * y_rows, :], fc_all)
        if d:
            ysend[d - 1] = part.astype(BF16)
            send("y", d, copy(ysend.at[d - 1], yrecv.at[d - 1], y_s.at[d - 1], y_r.at[d - 1], at_y(d)))
        else:
            yown[...] = part

    def pair_setup():
        for g in range(4):
            waits[("h", g)].wait_recv()
            waits[("hp", g)].wait_recv()
        own_t = jnp.transpose(feat_ref[...].astype(F32))
        ghost = jnp.concatenate([hfeat[...].reshape(4 * face, chan), jnp.zeros((atoms - 4 * face, chan), BF16)], axis=0)
        ghost_t = jnp.transpose(ghost.astype(F32))
        bufft[...] = jnp.concatenate([own_t, ghost_t], axis=1).astype(BF16)
        cott[...] = jnp.transpose(cot_ref[...].astype(F32))
        wradt[...] = jnp.transpose(
            jnp.concatenate([wrad_ref[...].astype(F32), jnp.zeros((128 - wrad_ref.shape[0], 128), F32)], axis=0)
        ).astype(BF16)
        woutt[...] = jnp.transpose(wout_ref[...].astype(F32)).astype(BF16)
        lane = lax.broadcasted_iota(jnp.int32, (8, atoms), 1)
        ghost_pos = jnp.zeros((8, atoms), F32)
        for g in range(4):
            moved = pltpu.roll(hpos[g], (face if g % 2 else atoms - face), axis=1)
            ghost_pos = jnp.where((lane >= g * face) & (lane < (g + 1) * face), moved, ghost_pos)
        possp[:, 0:atoms] = split3(gpos[0])
        possp[:, atoms : 2 * atoms] = split3(ghost_pos)
        for ref in (dbf, dbp, ownp, pwo, pwr):
            ref[...] = jnp.zeros(ref.shape, F32)

    levels = wrad_ref.shape[0]
    rates = 0.5 * jnp.exp(
        lax.broadcasted_iota(jnp.int32, (levels, 1), 0).astype(F32) * (math.log(16.0) / (levels - 1))
    )

    def pair_chunk(q):
        span = 2
        first = q * span
        idx = jnp.concatenate([nbr_ref[first + j : first + j + 1, :] for j in range(span)], axis=1)
        width = span * atoms
        hot = jnp.where(lax.broadcasted_iota(jnp.int32, (buf_rows, width), 0) == idx, 1.0, 0.0).astype(BF16)
        tp = nn(possp[:, 0:buf_rows], hot)
        target = tp[0:8] + tp[8:16] + tp[16:24]
        source = jnp.concatenate([gpos[0]] * span, axis=1)
        cosine, chord = turns(target - source)
        dist2 = jnp.sum(chord * chord, axis=0, keepdims=True)
        rbf = jnp.exp(-rates * dist2)
        rbf_h = rbf.astype(BF16)
        pre = nn(wradt[:, 0:levels], rbf_h)
        gate = 0.5 * jnp.tanh(0.5 * pre) + 0.5
        act = (pre * gate).astype(BF16)
        phi = nn(woutt[...], act)
        weight = jnp.concatenate(
            [cott[...] * jnp.where(cnt_ref[...] > first + j, slots**-0.5, 0.0) for j in range(span)], axis=1
        )
        given = weight * phi
        given_hi = given.astype(BF16)
        given_lo = (given - given_hi.astype(F32)).astype(BF16)
        added = nt(hot, jnp.concatenate([given_hi, given_lo], axis=0))
        dbf[...] += added[:, 0:chan] + added[:, chan : 2 * chan]
        dphi = (weight * nn(bufft[:, 0:buf_rows], hot)).astype(BF16)
        pwo[...] += nt(act, dphi)
        d_act = nn(wout_ref[...], dphi)
        dpre = (d_act * gate * (1.0 + pre * (1.0 - gate))).astype(BF16)
        pwr[...] += nt(rbf_h, dpre)
        d_rbf = nn(wrad_ref[...], dpre)
        d_chord2 = -jnp.sum(d_rbf * rates * rbf, axis=0, keepdims=True)
        dmove = (2.0 * mu) * d_chord2 * chord * cosine
        move_hi = dmove.astype(BF16).astype(F32)
        moves = nt(jnp.concatenate([move_hi, dmove - move_hi], axis=0).astype(BF16), hot)
        dbp[...] += moves[0:8] + moves[8:16]
        for j in range(span):
            ownp[...] -= dmove[:, j * atoms : (j + 1) * atoms]

    chunks = slots // 2
    cuts = [0, chunks * 3 // 8, chunks * 5 // 8, chunks * 7 // 8, chunks]
    pair_setup()
    for q in range(cuts[0], cuts[1]):
        pair_chunk(q)

    for d in range(1, N_Y):
        waits[("y", d)].wait_recv()
    z_rows = 2 * EDGE
    total = yown[...]
    for d in range(1, N_Y):
        total = total + yrecv[d - 1].astype(F32)
    z_order = sorted(range(1, n_z), key=lambda d: -min(d, n_z - d))
    for d in z_order:
        zsend[d - 1] = total[d * z_rows : (d + 1) * z_rows, :].astype(BF16)
        send("z", d, copy(zsend.at[d - 1], zrecv.at[d - 1], z_s.at[d - 1], z_r.at[d - 1], at_z(d)))
    mine = total[0:z_rows, :]
    for q in range(cuts[1], cuts[2]):
        pair_chunk(q)

    for d in range(1, n_z):
        waits[("z", d)].wait_recv()
        mine = mine + zrecv[d - 1].astype(F32)
    mine = nu * mine
    o_filter[...] = (
        mine[0:EDGE, 0:chan] * mine[0:EDGE, chan : 2 * chan]
        + mine[EDGE : 2 * EDGE, 0:chan] * mine[EDGE : 2 * EDGE, chan : 2 * chan]
    )
    load_filter.wait()
    kf = jnp.concatenate([kf8[...], kf8[...]], axis=0)
    wbuf[0, 0] = jnp.concatenate([kf * mine[:, chan : 2 * chan], kf * mine[:, 0:chan]], axis=1).astype(BF16)
    for d in z_order:
        there = n_z - d
        send("za", there, copy(wbuf.at[0, 0], wbuf.at[0, there], za_s.at[d - 1], za_r.at[there - 1], at_z(d)))
    for q in range(cuts[2], cuts[3]):
        pair_chunk(q)

    for d in range(1, n_z):
        waits[("za", d)].wait_recv()
    for d in y_order:
        there = N_Y - d
        send("ya", there, copy(wbuf.at[0], wbuf.at[there], ya_s.at[d - 1], ya_r.at[there - 1], at_y(d)))
    for q in range(cuts[3], cuts[4]):
        pair_chunk(q)

    dgp[...] = jnp.concatenate([dbp[:, atoms:buf_rows], jnp.zeros((8, 2 * atoms - buf_rows), F32)], axis=1)
    for g in range(4):
        send("rf", g, copy(dbf.at[pl.ds(atoms + g * face, face)], retf.at[g], rf_s.at[g], rf_r.at[g], at_dom[g]))
        send("rp", g, copy(dgp, retp.at[g], rp_s.at[g], rp_r.at[g], at_dom[g]))
    out_rows = pwo.shape[0] // group
    rad_rows = levels // group
    for j in range(group):
        pw_a[j, 0:out_rows] = pwo[j * out_rows : (j + 1) * out_rows, :]
        tail = pwr[j * rad_rows : (j + 1) * rad_rows, :]
        pw_a[j, out_rows:] = jnp.concatenate([tail, jnp.zeros((8 - rad_rows, tail.shape[1]), F32)], axis=0)
    my_piece = x * N_CORE + core
    for p in far_first:
        s = slot_of[p]
        piece = lax.rem(x + p[0], N_X) * N_CORE + lax.rem(core + p[1], N_CORE)
        send("pa", s, copy(pw_a.at[piece], pw_ar.at[s - 1], pa_s.at[s - 1], pa_r.at[s - 1], at_xc(*p)))

    for d in range(1, N_Y):
        waits[("ya", d)].wait_recv()
    w_all = wbuf[...].reshape(2 * k_loc, 2 * chan)
    fg_t = jnp.transpose(w_all[:, 0:chan].astype(F32)).astype(BF16)
    krow_h = krow[...].astype(BF16)

    def give_back(s):
        lanes = slice(s * atoms, (s + 1) * atoms)
        d_feat_t = nn(fg_t, csh[:, lanes])
        pq = nt(w_all, gfc[s]).reshape(-1, 2, EDGE, atoms)
        cs = csf[:, :, lanes].reshape(-1, 2, EDGE, atoms)
        wave = (cs[:, 0] * pq[:, 1] - cs[:, 1] * pq[:, 0]).reshape(k_loc, atoms)
        hi = wave.astype(BF16)
        lo = (wave - hi.astype(F32)).astype(BF16)
        d_pos = mu * (nn(krow_h, hi) + nn(krow_h, lo))
        return d_feat_t, d_pos

    for p in far_first:
        s = slot_of[p]
        d_feat_t, d_pos = give_back(s)
        outs_f[s - 1] = d_feat_t.astype(BF16)
        outs_p[s - 1] = d_pos
        home = at_xc((N_X - p[0]) % N_X, (N_CORE - p[1]) % N_CORE)
        send("of", s, copy(outs_f.at[s - 1], outr_f.at[s - 1], of_s.at[s - 1], of_r.at[s - 1], home))
        send("op", s, copy(outs_p.at[s - 1], outr_p.at[s - 1], op_s.at[s - 1], op_r.at[s - 1], home))

    for p in xc:
        waits[("pa", slot_of[p])].wait_recv()
    piece_sum = pw_a[my_piece]
    for s in range(group - 1):
        piece_sum = piece_sum + pw_ar[s]
    pw_b[...] = piece_sum
    for d in z_order:
        send("pb", d, copy(pw_b, pw_br.at[d - 1], pb_s.at[d - 1], pb_r.at[d - 1], at_z(d)))

    d_feat_t, d_pos = give_back(0)
    own_f[...] = d_feat_t
    own_p[...] = d_pos

    for d in range(1, n_z):
        waits[("pb", d)].wait_recv()
        piece_sum = piece_sum + pw_br[d - 1]
    pw_c[...] = piece_sum
    for d in y_order:
        send("pc", d, copy(pw_c, pw_cr.at[d - 1], pc_s.at[d - 1], pc_r.at[d - 1], at_y(d)))

    for g in range(4):
        waits[("rf", g)].wait_recv()
        waits[("rp", g)].wait_recv()
    lane = lax.broadcasted_iota(jnp.int32, (8, atoms), 1)
    short_pos = dbp[:, 0:atoms] + ownp[...]
    for g in range(4):
        f = g ^ 1
        moved = pltpu.roll(retp[g], (atoms - face if g % 2 else face), axis=1)
        short_pos = short_pos + jnp.where((lane >= f * face) & (lane < (f + 1) * face), moved, 0.0)

    for d in range(1, N_Y):
        waits[("pc", d)].wait_recv()
        piece_sum = piece_sum + pw_cr[d - 1]
    pw_d[my_piece] = nu * piece_sum
    for p in far_first:
        s = slot_of[p]
        send("pd", s, copy(pw_d.at[my_piece], pw_d.at[my_piece], pd_s.at[s - 1], pd_r.at[s - 1], at_xc(*p)))

    long_t = own_f[...]
    long_pos = own_p[...]
    for p in near_first:
        s = slot_of[p]
        waits[("of", s)].wait_recv()
        waits[("op", s)].wait_recv()
        long_t = long_t + outr_f[s - 1].astype(F32)
        long_pos = long_pos + outr_p[s - 1]
    long_feat = jnp.transpose(long_t)
    for g in range(4):
        f = g ^ 1
        rows = slice(f * face, (f + 1) * face)
        o_feat[rows, :] = long_feat[rows] + dbf[rows, :] + retf[g]
    o_feat[4 * face :, :] = long_feat[4 * face :] + dbf[4 * face : atoms, :]
    o_pos[...] = (long_pos + short_pos)[0:3]

    for p in xc:
        waits[("pd", slot_of[p])].wait_recv()
    for j in range(group):
        o_out[j * out_rows : (j + 1) * out_rows, :] = pw_d[j, 0:out_rows]
        o_radial[j * rad_rows : (j + 1) * rad_rows, :] = pw_d[j, out_rows : out_rows + rad_rows]
    for c in sent:
        c.wait_send()


def shards(features, cotangent, positions, neighbours, counts, k_index, k_filter, w_radial, w_out):
    n_slab = lax.axis_size("slab")
    atoms, chan = features.shape
    levels, hidden = w_radial.shape
    group = N_X * N_CORE
    n_z = Z_HI * n_slab
    k_loc = N_Y * n_z * EDGE
    face = atoms // 8
    buf_rows = atoms + 4 * face
    piece = hidden // group + 8
    v = pltpu.VMEM
    dma = pltpu.SemaphoreType.DMA
    vmem = pl.BlockSpec(memory_space=pltpu.VMEM)
    scratch = [
        v((group, atoms, 2 * chan), BF16),
        v((group, 8, atoms), F32),
        v((4, face, chan), BF16),
        v((4, 8, atoms), F32),
        v((2 * k_loc // EDGE, EDGE, group * atoms), F32),
        v((2 * k_loc, group * atoms), BF16),
        v((N_Y - 1, 2 * n_z * EDGE, 2 * chan), BF16),
        v((2 * n_z * EDGE, 2 * chan), F32),
        v((N_Y - 1, 2 * n_z * EDGE, 2 * chan), BF16),
        v((n_z - 1, 2 * EDGE, 2 * chan), BF16),
        v((n_z - 1, 2 * EDGE, 2 * chan), BF16),
        v((N_Y, n_z, 2 * EDGE, 2 * chan), BF16),
        v((EDGE, chan), F32),
        v((group - 1, chan, atoms), BF16),
        v((group - 1, 8, atoms), F32),
        v((group - 1, chan, atoms), BF16),
        v((group - 1, 8, atoms), F32),
        v((chan, atoms), F32),
        v((8, atoms), F32),
        v((k_loc, 32), BF16),
        v((8, k_loc), F32),
        v((chan, 2 * atoms), BF16),
        v((32, 2 * atoms), BF16),
        v((chan, atoms), F32),
        v((hidden, 128), BF16),
        v((chan, hidden), BF16),
        v((buf_rows, chan), F32),
        v((8, buf_rows), F32),
        v((8, atoms), F32),
        v((8, atoms), F32),
        v((hidden, chan), F32),
        v((levels, hidden), F32),
        v((4, face, chan), F32),
        v((4, 8, atoms), F32),
        v((group, piece, chan), F32),
        v((group - 1, piece, chan), F32),
        v((piece, chan), F32),
        v((n_z - 1, piece, chan), F32),
        v((piece, chan), F32),
        v((N_Y - 1, piece, chan), F32),
        v((group, piece, chan), F32),
        dma,
    ]
    for n in (group - 1, group - 1, 4, 4, N_Y - 1, n_z - 1, n_z - 1, N_Y - 1):
        scratch += [dma((n,)), dma((n,))]
    for n in (group - 1, group - 1, 4, 4, group - 1, n_z - 1, N_Y - 1, group - 1):
        scratch += [dma((n,)), dma((n,))]
    return pl.pallas_call(
        functools.partial(body, n_slab),
        out_shape=(
            jax.ShapeDtypeStruct((atoms, chan), F32),
            jax.ShapeDtypeStruct((3, atoms), F32),
            jax.ShapeDtypeStruct((EDGE, chan), F32),
            jax.ShapeDtypeStruct((levels, hidden), F32),
            jax.ShapeDtypeStruct((hidden, chan), F32),
        ),
        in_specs=[vmem] * 6 + [pl.BlockSpec(memory_space=pl.ANY)] + [vmem] * 2,
        out_specs=(vmem,) * 5,
        scratch_shapes=scratch,
        compiler_params=pltpu.CompilerParams(
            collective_id=0, has_side_effects=True, vmem_limit_bytes=40 << 20
        ),
        name="ewald",
    )(
        features,
        cotangent,
        positions,
        neighbours,
        counts.reshape(1, atoms),
        k_index,
        k_filter,
        w_radial,
        w_out,
    )


def solution(mesh):
    both = ("dom", "slab")
    in_specs = (P(both, None), P(both, None), P(None, both), P(None, both), P(both), P(), P(), P(), P())
    out_specs = (P(both, None), P(None, both), P(both, None), P(), P())
    return jax.shard_map(shards, mesh=mesh, in_specs=in_specs, out_specs=out_specs, check_vma=False)
```

```python
import functools
import math

import jax
import jax.numpy as jnp
from jax import lax
from jax.experimental import pallas as pl
from jax.experimental.pallas import tpu as pltpu
from jax.sharding import PartitionSpec as P

Z_HI, N_X, N_Y, N_CORE = 2, 4, 4, 2
EDGE = 8
PART = 6
F32 = jnp.float32
BF16 = jnp.bfloat16

SIN_C = (3.1415926401307077, -5.167710083507896, 2.550077523214726, -0.5982912856213906, 0.07765766030763246)
COS_C = (
    0.9999999997799044,
    -4.934802137078806,
    4.058709159555702,
    -1.3352120030438075,
    0.23493731378604543,
    -0.024396324301093893,
)


def horner(coefs, u):
    y = coefs[-1] * u + coefs[-2]
    for k in coefs[-3::-1]:
        y = y * u + k
    return y


def turns(t):
    r = t - jnp.round(t)
    u = r * r
    s = r * horner(SIN_C, u)
    c = horner(COS_C, u)
    return 1.0 - 2.0 * (s * s), 2.0 * (s * c)


def split3(v):
    hi = v.astype(BF16)
    rest = v - hi.astype(F32)
    mid = rest.astype(BF16)
    lo = (rest - mid.astype(F32)).astype(BF16)
    return jnp.concatenate([hi.astype(F32), mid.astype(F32), lo.astype(F32), jnp.zeros_like(v)], axis=0).astype(BF16)


def nn(a, b):
    return lax.dot_general(a, b, (((1,), (0,)), ((), ())), preferred_element_type=F32)


def nt(a, b):
    return lax.dot_general(a, b, (((1,), (1,)), ((), ())), preferred_element_type=F32)


def body(
    n_slab,
    feat_hbm,
    cot_hbm,
    pos_hbm,
    nbr_hbm,
    cnt_hbm,
    kidx_hbm,
    kfil_hbm,
    wrad_hbm,
    wout_hbm,
    feat_out,
    pos_out,
    filter_out,
    radial_out,
    out_out,
    o_feat,
    o_pos,
    o_filter,
    o_radial,
    o_out,
    pos_ref,
    nbr_ref,
    cnt_ref,
    kidx_ref,
    wrad_ref,
    wout_ref,
    gfc,
    gpos,
    hfeat,
    hpos,
    csf,
    csh,
    ysend,
    yown,
    yrecv,
    zsend,
    zrecv,
    wbuf,
    kf8,
    outs_f,
    outs_p,
    outr_f,
    outr_p,
    kcol,
    krow,
    bufft,
    possp,
    cott,
    wradt,
    woutt,
    dbf,
    dbp,
    dgp,
    ownp,
    pwo,
    pwr,
    retf,
    retp,
    pw_a,
    pw_ar,
    pw_b,
    pw_br,
    pw_c,
    pw_cr,
    pw_d,
    loc_sem,
    st_sem,
    g_s,
    g_r,
    gp_s,
    gp_r,
    h_s,
    h_r,
    hp_s,
    hp_r,
    y_s,
    y_r,
    z_s,
    z_r,
    za_s,
    za_r,
    ya_s,
    ya_r,
    of_s,
    of_r,
    op_s,
    op_r,
    rf_s,
    rf_r,
    rp_s,
    rp_r,
    pa_s,
    pa_r,
    pb_s,
    pb_r,
    pc_s,
    pc_r,
    pd_s,
    pd_r,
):
    atoms, chan = feat_hbm.shape
    slots = nbr_ref.shape[0]
    k_total = kidx_ref.shape[1]
    n_z = Z_HI * n_slab
    group = N_X * N_CORE
    k_loc = N_Y * n_z * EDGE
    n_dom = Z_HI * N_X * N_Y * N_CORE
    face = atoms // 8
    buf_rows = atoms + 4 * face
    nu = 1.0 / math.sqrt(atoms * n_dom * n_slab)
    mu = 1.0 / math.sqrt(k_total)

    dom = lax.axis_index("dom")
    slab = lax.axis_index("slab")
    core = lax.rem(dom, N_CORE)
    y = lax.rem(lax.div(dom, N_CORE), N_Y)
    x = lax.rem(lax.div(dom, N_CORE * N_Y), N_X)
    zh = lax.div(dom, N_CORE * N_Y * N_X)
    z = zh * n_slab + slab

    def dom_of(zh_, x_, y_, c_):
        return ((zh_ * N_X + x_) * N_Y + y_) * N_CORE + c_

    def at_xc(dx, dc):
        return (dom_of(zh, lax.rem(x + dx, N_X), y, lax.rem(core + dc, N_CORE)), slab)

    def at_y(d):
        return (dom_of(zh, x, lax.rem(y + d, N_Y), core), slab)

    def at_z(d):
        zz = lax.rem(z + d, n_z)
        return (dom_of(lax.div(zz, n_slab), x, y, core), lax.rem(zz, n_slab))

    at_dom = (
        (lax.rem(dom + n_dom - 1, n_dom), slab),
        (lax.rem(dom + 1, n_dom), slab),
        (dom, lax.rem(slab + n_slab - 1, n_slab)),
        (dom, lax.rem(slab + 1, n_slab)),
    )

    def copy(src, dst, ss, rs, dev):
        return pltpu.make_async_remote_copy(
            src_ref=src, dst_ref=dst, send_sem=ss, recv_sem=rs, device_id=dev, device_id_type=pl.DeviceIdType.MESH
        )

    xc = [(dx, dc) for dx in range(N_X) for dc in range(N_CORE)][1:]
    slot_of = {p: p[0] * N_CORE + p[1] for p in xc}
    far_first = sorted(xc, key=lambda p: -min(p[0], N_X - p[0]))
    near_first = far_first[::-1]

    peers = [at_xc(*p) for p in xc] + [at_y(d) for d in range(1, N_Y)] + [at_z(d) for d in range(1, n_z)]
    peers += [at_dom[0], at_dom[1]]
    barrier = pltpu.get_barrier_semaphore()
    for dev in peers:
        pl.semaphore_signal(barrier, inc=1, device_id=dev, device_id_type=pl.DeviceIdType.MESH)

    k_first = pl.multiple_of((dom * n_slab + slab) * EDGE, EDGE)
    results = {
        name: pltpu.make_async_copy(src, dst, st_sem.at[i])
        for i, (name, src, dst) in enumerate(
            (
                ("feat", o_feat, feat_out),
                ("pos", o_pos, pos_out),
                ("filter", o_filter, filter_out),
                ("radial", o_radial, radial_out),
                ("out", o_out, out_out),
            )
        )
    }
    loads = {}
    for i, (name, src, dst) in enumerate(
        (
            ("pos", pos_hbm, pos_ref),
            ("feat", feat_hbm, gfc.at[0, :, pl.ds(0, chan)]),
            ("cot", cot_hbm, gfc.at[0, :, pl.ds(chan, chan)]),
            ("kidx", kidx_hbm, kidx_ref),
            ("nbr", nbr_hbm, nbr_ref),
            ("cnt", cnt_hbm, cnt_ref),
            ("wrad", wrad_hbm, wrad_ref),
            ("wout", wout_hbm, wout_ref),
            ("filter", kfil_hbm.at[pl.ds(k_first, EDGE)], kf8),
        )
    ):
        loads[name] = pltpu.make_async_copy(src, dst, loc_sem.at[i])
        loads[name].start()
    gpos[0] = jnp.zeros((8, atoms), F32)
    loads["pos"].wait()
    gpos[0, 0:3] = pos_ref[...]

    pl.semaphore_wait(barrier, len(peers))

    sent = []
    waits = {}

    def send(name, key, c):
        c.start()
        sent.append(c)
        waits[(name, key)] = c

    for p in far_first:
        s = slot_of[p]
        send("gp", s, copy(gpos.at[0], gpos.at[s], gp_s.at[s - 1], gp_r.at[s - 1], at_xc(*p)))
    loads["feat"].wait()
    loads["cot"].wait()
    for p in far_first:
        s = slot_of[p]
        send("g", s, copy(gfc.at[0], gfc.at[s], g_s.at[s - 1], g_r.at[s - 1], at_xc(*p)))
    for g in range(4):
        f = g ^ 1
        dev = at_dom[f]
        mine = gfc.at[0, pl.ds(f * face, face), pl.ds(0, chan)]
        send("h", g, copy(mine, hfeat.at[g], h_s.at[g], h_r.at[g], dev))
        send("hp", g, copy(gpos.at[0], hpos.at[g], hp_s.at[g], hp_r.at[g], dev))
    loads["kidx"].wait()

    m = lax.broadcasted_iota(jnp.int32, (k_loc, k_total), 0)
    e = jnp.bitwise_and(m, EDGE - 1)
    bz = lax.rem(lax.div(m, EDGE) + z, n_z)
    by = lax.rem(lax.div(m, EDGE * n_z) + y, N_Y)
    row = (dom_of(lax.div(bz, n_slab), x, by, core) * n_slab + lax.rem(bz, n_slab)) * EDGE + e
    pick = jnp.where(row == lax.broadcasted_iota(jnp.int32, (k_loc, k_total), 1), 1.0, 0.0).astype(BF16)
    k8 = jnp.concatenate([kidx_ref[...].astype(F32), jnp.zeros((5, k_total), F32)], axis=0)
    krow[...] = nt(k8.astype(BF16), pick)
    kcol[...] = nt(pick, jnp.concatenate([k8, k8, k8, jnp.zeros_like(k8)], axis=0).astype(BF16)).astype(BF16)

    def tables(s):
        t = nn(kcol[...], split3(gpos[s]))
        cosine, sine = turns(t)
        lanes = slice(s * atoms, (s + 1) * atoms)
        both = jnp.stack([cosine.reshape(-1, EDGE, atoms), sine.reshape(-1, EDGE, atoms)], axis=1)
        csf[:, :, lanes] = both.reshape(-1, EDGE, atoms)
        csh[:, lanes] = both.reshape(-1, atoms).astype(BF16)

    tables(0)
    for p in near_first:
        s = slot_of[p]
        waits[("gp", s)].wait_recv()
        tables(s)
    for p in near_first:
        waits[("g", slot_of[p])].wait_recv()

    fc_all = gfc[...].reshape(group * atoms, 2 * chan)
    y_rows = n_z * 2 * EDGE
    y_order = sorted(range(1, N_Y), key=lambda d: -min(d, N_Y - d))
    for d in y_order + [0]:
        part = nn(csh[d * y_rows : (d + 1) * y_rows, :], fc_all)
        if d:
            ysend[d - 1] = part.astype(BF16)
            send("y", d, copy(ysend.at[d - 1], yrecv.at[d - 1], y_s.at[d - 1], y_r.at[d - 1], at_y(d)))
        else:
            yown[...] = part

    def pair_setup():
        for g in range(4):
            waits[("h", g)].wait_recv()
            waits[("hp", g)].wait_recv()
        for name in ("nbr", "cnt", "wrad", "wout"):
            loads[name].wait()
        own_t = jnp.transpose(gfc[0, :, 0:chan].astype(F32))
        ghost = jnp.concatenate([hfeat[...].reshape(4 * face, chan), jnp.zeros((atoms - 4 * face, chan), BF16)], axis=0)
        ghost_t = jnp.transpose(ghost.astype(F32))
        bufft[...] = jnp.concatenate([own_t, ghost_t], axis=1).astype(BF16)
        cott[...] = jnp.transpose(gfc[0, :, chan : 2 * chan].astype(F32))
        wradt[...] = jnp.transpose(
            jnp.concatenate([wrad_ref[...].astype(F32), jnp.zeros((128 - wrad_ref.shape[0], 128), F32)], axis=0)
        ).astype(BF16)
        woutt[...] = jnp.transpose(wout_ref[...].astype(F32)).astype(BF16)
        lane = lax.broadcasted_iota(jnp.int32, (8, atoms), 1)
        ghost_pos = jnp.zeros((8, atoms), F32)
        for g in range(4):
            moved = pltpu.roll(hpos[g], (face if g % 2 else atoms - face), axis=1)
            ghost_pos = jnp.where((lane >= g * face) & (lane < (g + 1) * face), moved, ghost_pos)
        possp[:, 0:atoms] = split3(gpos[0])
        possp[:, atoms : 2 * atoms] = split3(ghost_pos)
        for ref in (dbf, dbp, ownp, pwo, pwr):
            ref[...] = jnp.zeros(ref.shape, F32)

    levels = wrad_ref.shape[0]
    rates = 0.5 * jnp.exp(
        lax.broadcasted_iota(jnp.int32, (levels, 1), 0).astype(F32) * (math.log(16.0) / (levels - 1))
    )

    def pair_chunk(q):
        span = 2
        first = q * span
        idx = jnp.concatenate([nbr_ref[first + j : first + j + 1, :] for j in range(span)], axis=1)
        width = span * atoms
        hot = jnp.where(lax.broadcasted_iota(jnp.int32, (buf_rows, width), 0) == idx, 1.0, 0.0).astype(BF16)
        tp = nn(possp[:, 0:buf_rows], hot)
        target = tp[0:8] + tp[8:16] + tp[16:24]
        source = jnp.concatenate([gpos[0]] * span, axis=1)
        cosine, chord = turns(target - source)
        dist2 = jnp.sum(chord * chord, axis=0, keepdims=True)
        rbf = jnp.exp(-rates * dist2)
        rbf_h = rbf.astype(BF16)
        pre = nn(wradt[:, 0:levels], rbf_h)
        gate = 0.5 * jnp.tanh(0.5 * pre) + 0.5
        act = (pre * gate).astype(BF16)
        phi = nn(woutt[...], act)
        weight = jnp.concatenate(
            [cott[...] * jnp.where(cnt_ref[...] > first + j, slots**-0.5, 0.0) for j in range(span)], axis=1
        )
        given = weight * phi
        given_hi = given.astype(BF16)
        given_lo = (given - given_hi.astype(F32)).astype(BF16)
        added = nt(hot, jnp.concatenate([given_hi, given_lo], axis=0))
        dbf[...] += added[:, 0:chan] + added[:, chan : 2 * chan]
        dphi = (weight * nn(bufft[:, 0:buf_rows], hot)).astype(BF16)
        pwo[...] += nt(act, dphi)
        d_act = nn(wout_ref[...], dphi)
        dpre = (d_act * gate * (1.0 + pre * (1.0 - gate))).astype(BF16)
        pwr[...] += nt(rbf_h, dpre)
        d_rbf = nn(wrad_ref[...], dpre)
        d_chord2 = -jnp.sum(d_rbf * rates * rbf, axis=0, keepdims=True)
        dmove = (2.0 * mu) * d_chord2 * chord * cosine
        move_hi = dmove.astype(BF16).astype(F32)
        moves = nt(jnp.concatenate([move_hi, dmove - move_hi], axis=0).astype(BF16), hot)
        dbp[...] += moves[0:8] + moves[8:16]
        for j in range(span):
            ownp[...] -= dmove[:, j * atoms : (j + 1) * atoms]

    out_rows = pwo.shape[0] // group
    rad_rows = levels // group
    my_piece = x * N_CORE + core

    def pair_sends():
        for j in range(group):
            pw_a[j, 0:out_rows] = pwo[j * out_rows : (j + 1) * out_rows, :]
            tail = pwr[j * rad_rows : (j + 1) * rad_rows, :]
            pw_a[j, out_rows:] = jnp.concatenate([tail, jnp.zeros((8 - rad_rows, tail.shape[1]), F32)], axis=0)
        for p in far_first:
            s = slot_of[p]
            piece = lax.rem(x + p[0], N_X) * N_CORE + lax.rem(core + p[1], N_CORE)
            send("pa", s, copy(pw_a.at[piece], pw_ar.at[s - 1], pa_s.at[s - 1], pa_r.at[s - 1], at_xc(*p)))
        dgp[...] = jnp.concatenate([dbp[:, atoms:buf_rows], jnp.zeros((8, 2 * atoms - buf_rows), F32)], axis=1)
        for g in range(4):
            send("rf", g, copy(dbf.at[pl.ds(atoms + g * face, face)], retf.at[g], rf_s.at[g], rf_r.at[g], at_dom[g]))
            send("rp", g, copy(dgp, retp.at[g], rp_s.at[g], rp_r.at[g], at_dom[g]))

    chunks = slots // 2
    first_part = chunks * PART // 8
    pair_setup()
    for q in range(first_part):
        pair_chunk(q)
    if first_part == chunks:
        pair_sends()

    for d in range(1, N_Y):
        waits[("y", d)].wait_recv()
    z_rows = 2 * EDGE
    total = yown[...]
    for d in range(1, N_Y):
        total = total + yrecv[d - 1].astype(F32)
    z_order = sorted(range(1, n_z), key=lambda d: -min(d, n_z - d))
    for d in z_order:
        zsend[d - 1] = total[d * z_rows : (d + 1) * z_rows, :].astype(BF16)
        send("z", d, copy(zsend.at[d - 1], zrecv.at[d - 1], z_s.at[d - 1], z_r.at[d - 1], at_z(d)))
    mine = total[0:z_rows, :]
    for q in range(first_part, chunks):
        pair_chunk(q)
    if first_part < chunks:
        pair_sends()

    for d in range(1, n_z):
        waits[("z", d)].wait_recv()
        mine = mine + zrecv[d - 1].astype(F32)
    mine = nu * mine
    loads["filter"].wait()
    kf = jnp.concatenate([kf8[...], kf8[...]], axis=0)
    wbuf[0, 0] = jnp.concatenate([kf * mine[:, chan : 2 * chan], kf * mine[:, 0:chan]], axis=1).astype(BF16)
    for d in z_order:
        there = n_z - d
        send("za", there, copy(wbuf.at[0, 0], wbuf.at[0, there], za_s.at[d - 1], za_r.at[there - 1], at_z(d)))
    o_filter[...] = (
        mine[0:EDGE, 0:chan] * mine[0:EDGE, chan : 2 * chan]
        + mine[EDGE : 2 * EDGE, 0:chan] * mine[EDGE : 2 * EDGE, chan : 2 * chan]
    )
    results["filter"].start()

    for p in xc:
        waits[("pa", slot_of[p])].wait_recv()
    piece_sum = pw_a[my_piece]
    for s in range(group - 1):
        piece_sum = piece_sum + pw_ar[s]
    pw_b[...] = piece_sum

    for g in range(4):
        waits[("rf", g)].wait_recv()
        waits[("rp", g)].wait_recv()
    lane = lax.broadcasted_iota(jnp.int32, (8, atoms), 1)
    short_pos = dbp[:, 0:atoms] + ownp[...]
    for g in range(4):
        f = g ^ 1
        moved = pltpu.roll(retp[g], (atoms - face if g % 2 else face), axis=1)
        short_pos = short_pos + jnp.where((lane >= f * face) & (lane < (f + 1) * face), moved, 0.0)
        rows = slice(f * face, (f + 1) * face)
        dbf[rows, :] += retf[g]
    ownp[...] = short_pos

    for d in range(1, n_z):
        waits[("za", d)].wait_recv()
    for d in y_order:
        there = N_Y - d
        send("ya", there, copy(wbuf.at[0], wbuf.at[there], ya_s.at[d - 1], ya_r.at[there - 1], at_y(d)))
    for d in z_order:
        send("pb", d, copy(pw_b, pw_br.at[d - 1], pb_s.at[d - 1], pb_r.at[d - 1], at_z(d)))

    for d in range(1, N_Y):
        waits[("ya", d)].wait_recv()
    for d in range(1, n_z):
        waits[("pb", d)].wait_recv()
        piece_sum = piece_sum + pw_br[d - 1]
    pw_c[...] = piece_sum
    for d in y_order:
        send("pc", d, copy(pw_c, pw_cr.at[d - 1], pc_s.at[d - 1], pc_r.at[d - 1], at_y(d)))
    w_all = wbuf[...].reshape(2 * k_loc, 2 * chan)
    fg_t = jnp.transpose(w_all[:, 0:chan].astype(F32)).astype(BF16)
    krow_h = krow[...].astype(BF16)

    def give_back(s):
        lanes = slice(s * atoms, (s + 1) * atoms)
        d_feat_t = nn(fg_t, csh[:, lanes])
        pq = nt(w_all, gfc[s]).reshape(-1, 2, EDGE, atoms)
        cs = csf[:, :, lanes].reshape(-1, 2, EDGE, atoms)
        wave = (cs[:, 0] * pq[:, 1] - cs[:, 1] * pq[:, 0]).reshape(k_loc, atoms)
        hi = wave.astype(BF16)
        lo = (wave - hi.astype(F32)).astype(BF16)
        d_pos = mu * (nn(krow_h, hi) + nn(krow_h, lo))
        return d_feat_t, d_pos

    for p in far_first:
        s = slot_of[p]
        d_feat_t, d_pos = give_back(s)
        outs_f[s - 1] = d_feat_t.astype(BF16)
        outs_p[s - 1] = d_pos
        home = at_xc((N_X - p[0]) % N_X, (N_CORE - p[1]) % N_CORE)
        send("of", s, copy(outs_f.at[s - 1], outr_f.at[s - 1], of_s.at[s - 1], of_r.at[s - 1], home))
        send("op", s, copy(outs_p.at[s - 1], outr_p.at[s - 1], op_s.at[s - 1], op_r.at[s - 1], home))

    for d in range(1, N_Y):
        waits[("pc", d)].wait_recv()
        piece_sum = piece_sum + pw_cr[d - 1]
    pw_d[my_piece] = nu * piece_sum
    for p in far_first:
        s = slot_of[p]
        send("pd", s, copy(pw_d.at[my_piece], pw_d.at[my_piece], pd_s.at[s - 1], pd_r.at[s - 1], at_xc(*p)))

    long_t, long_pos = give_back(0)
    for p in near_first:
        s = slot_of[p]
        waits[("of", s)].wait_recv()
        waits[("op", s)].wait_recv()
        long_t = long_t + outr_f[s - 1].astype(F32)
        long_pos = long_pos + outr_p[s - 1]
    o_feat[...] = jnp.transpose(long_t) + dbf[0:atoms, :]
    o_pos[...] = (long_pos + ownp[...])[0:3]
    results["feat"].start()
    results["pos"].start()

    for p in xc:
        waits[("pd", slot_of[p])].wait_recv()
    for j in range(group):
        o_out[j * out_rows : (j + 1) * out_rows, :] = pw_d[j, 0:out_rows]
        o_radial[j * rad_rows : (j + 1) * rad_rows, :] = pw_d[j, out_rows : out_rows + rad_rows]
    results["out"].start()
    results["radial"].start()
    for c in sent:
        c.wait_send()
    for c in results.values():
        c.wait()


def store(*refs):
    n = len(refs) // 2
    sem = refs[-1]
    moves = [pltpu.make_async_copy(refs[i], refs[n + i], sem.at[i]) for i in range(n)]
    for c in moves:
        c.start()
    for c in moves:
        c.wait()


def shards(features, cotangent, positions, neighbours, counts, k_index, k_filter, w_radial, w_out):
    n_slab = lax.axis_size("slab")
    atoms, chan = features.shape
    levels, hidden = w_radial.shape
    group = N_X * N_CORE
    n_z = Z_HI * n_slab
    k_loc = N_Y * n_z * EDGE
    face = atoms // 8
    buf_rows = atoms + 4 * face
    piece = hidden // group + 8
    v = pltpu.VMEM
    dma = pltpu.SemaphoreType.DMA
    scratch = [
        v((atoms, chan), F32),
        v((3, atoms), F32),
        v((EDGE, chan), F32),
        v((levels, hidden), F32),
        v((hidden, chan), F32),
        v(positions.shape, F32),
        v(neighbours.shape, jnp.int32),
        v((1, atoms), jnp.int32),
        v(k_index.shape, jnp.int32),
        v(w_radial.shape, BF16),
        v(w_out.shape, BF16),
        v((group, atoms, 2 * chan), BF16),
        v((group, 8, atoms), F32),
        v((4, face, chan), BF16),
        v((4, 8, atoms), F32),
        v((2 * k_loc // EDGE, EDGE, group * atoms), F32),
        v((2 * k_loc, group * atoms), BF16),
        v((N_Y - 1, 2 * n_z * EDGE, 2 * chan), BF16),
        v((2 * n_z * EDGE, 2 * chan), F32),
        v((N_Y - 1, 2 * n_z * EDGE, 2 * chan), BF16),
        v((n_z - 1, 2 * EDGE, 2 * chan), BF16),
        v((n_z - 1, 2 * EDGE, 2 * chan), BF16),
        v((N_Y, n_z, 2 * EDGE, 2 * chan), BF16),
        v((EDGE, chan), F32),
        v((group - 1, chan, atoms), BF16),
        v((group - 1, 8, atoms), F32),
        v((group - 1, chan, atoms), BF16),
        v((group - 1, 8, atoms), F32),
        v((k_loc, 32), BF16),
        v((8, k_loc), F32),
        v((chan, 2 * atoms), BF16),
        v((32, 2 * atoms), BF16),
        v((chan, atoms), F32),
        v((hidden, 128), BF16),
        v((chan, hidden), BF16),
        v((buf_rows, chan), F32),
        v((8, buf_rows), F32),
        v((8, atoms), F32),
        v((8, atoms), F32),
        v((hidden, chan), F32),
        v((levels, hidden), F32),
        v((4, face, chan), F32),
        v((4, 8, atoms), F32),
        v((group, piece, chan), F32),
        v((group - 1, piece, chan), F32),
        v((piece, chan), F32),
        v((n_z - 1, piece, chan), F32),
        v((piece, chan), F32),
        v((N_Y - 1, piece, chan), F32),
        v((group, piece, chan), F32),
        dma((9,)),
        dma((5,)),
    ]
    for n in (group - 1, group - 1, 4, 4, N_Y - 1, n_z - 1, n_z - 1, N_Y - 1):
        scratch += [dma((n,)), dma((n,))]
    for n in (group - 1, group - 1, 4, 4, group - 1, n_z - 1, N_Y - 1, group - 1):
        scratch += [dma((n,)), dma((n,))]
    hbm = pl.BlockSpec(memory_space=pltpu.HBM)
    shapes = (
        jax.ShapeDtypeStruct((atoms, chan), F32),
        jax.ShapeDtypeStruct((3, atoms), F32),
        jax.ShapeDtypeStruct((EDGE, chan), F32),
        jax.ShapeDtypeStruct((levels, hidden), F32),
        jax.ShapeDtypeStruct((hidden, chan), F32),
    )
    results = pl.pallas_call(
        functools.partial(body, n_slab),
        out_shape=shapes,
        in_specs=[hbm] * 9,
        out_specs=(hbm,) * 5,
        scratch_shapes=scratch,
        compiler_params=pltpu.CompilerParams(
            collective_id=0, has_side_effects=True, vmem_limit_bytes=56 << 20
        ),
        name="ewald",
    )(
        features,
        cotangent,
        positions,
        neighbours,
        counts.reshape(1, atoms),
        k_index,
        k_filter,
        w_radial,
        w_out,
    )
    return pl.pallas_call(
        store,
        out_shape=shapes,
        in_specs=[hbm] * 5,
        out_specs=(hbm,) * 5,
        scratch_shapes=[dma((5,))],
        compiler_params=pltpu.CompilerParams(vmem_limit_bytes=56 << 20),
        name="store",
    )(*results)


def solution(mesh):
    both = ("dom", "slab")
    in_specs = (P(both, None), P(both, None), P(None, both), P(None, both), P(both), P(), P(), P(), P())
    out_specs = (P(both, None), P(None, both), P(both, None), P(), P())
    return jax.shard_map(shards, mesh=mesh, in_specs=in_specs, out_specs=out_specs, check_vma=False)
```

```python
import functools
import math

import jax
import jax.numpy as jnp
from jax import lax
from jax.experimental import pallas as pl
from jax.experimental.pallas import tpu as pltpu
from jax.sharding import PartitionSpec as P

Z_HI, N_X, N_Y, N_CORE = 2, 4, 4, 2
EDGE = 8
PART = 6
NEAR = 5
F32 = jnp.float32
BF16 = jnp.bfloat16

SIN_C = (3.1415926401307077, -5.167710083507896, 2.550077523214726, -0.5982912856213906, 0.07765766030763246)
COS_C = (
    0.9999999997799044,
    -4.934802137078806,
    4.058709159555702,
    -1.3352120030438075,
    0.23493731378604543,
    -0.024396324301093893,
)


def horner(coefs, u):
    y = coefs[-1] * u + coefs[-2]
    for k in coefs[-3::-1]:
        y = y * u + k
    return y


def turns(t):
    r = t - jnp.round(t)
    u = r * r
    s = r * horner(SIN_C, u)
    c = horner(COS_C, u)
    return 1.0 - 2.0 * (s * s), 2.0 * (s * c)


def split3(v):
    hi = v.astype(BF16)
    rest = v - hi.astype(F32)
    mid = rest.astype(BF16)
    lo = (rest - mid.astype(F32)).astype(BF16)
    return jnp.concatenate([hi.astype(F32), mid.astype(F32), lo.astype(F32), jnp.zeros_like(v)], axis=0).astype(BF16)


def nn(a, b):
    return lax.dot_general(a, b, (((1,), (0,)), ((), ())), preferred_element_type=F32)


def nt(a, b):
    return lax.dot_general(a, b, (((1,), (1,)), ((), ())), preferred_element_type=F32)


def body(
    n_slab,
    feat_hbm,
    cot_hbm,
    pos_hbm,
    nbr_hbm,
    cnt_hbm,
    kidx_hbm,
    kfil_hbm,
    wrad_hbm,
    wout_hbm,
    feat_out,
    pos_out,
    filter_out,
    radial_out,
    out_out,
    o_feat,
    o_pos,
    o_filter,
    o_radial,
    o_out,
    pos_ref,
    nbr_ref,
    cnt_ref,
    kidx_ref,
    wrad_ref,
    wout_ref,
    gfc,
    gpos,
    hfeat,
    hpos,
    csf,
    csh,
    ysend,
    yown,
    yrecv,
    zsend,
    zrecv,
    wbuf,
    kf8,
    picked,
    gfct,
    hot_s,
    act_s,
    dpre_s,
    rbf_s,
    chord_s,
    cosine_s,
    pacc,
    facc,
    xacc,
    outs_c,
    outr_c,
    outs_x,
    outr_x,
    kcol,
    krow,
    bufft,
    possp,
    cott,
    wradt,
    woutt,
    dbf,
    dbp,
    dgp,
    ownp,
    pwo,
    pwr,
    retf,
    retp,
    pw_a,
    pw_ar,
    pw_b,
    pw_br,
    pw_c,
    pw_cr,
    pw_d,
    loc_sem,
    st_sem,
    g_s,
    g_r,
    gp_s,
    gp_r,
    h_s,
    h_r,
    hp_s,
    hp_r,
    y_s,
    y_r,
    z_s,
    z_r,
    za_s,
    za_r,
    ya_s,
    ya_r,
    oc_s,
    oc_r,
    ox_s,
    ox_r,
    rf_s,
    rf_r,
    rp_s,
    rp_r,
    pa_s,
    pa_r,
    pb_s,
    pb_r,
    pc_s,
    pc_r,
    pd_s,
    pd_r,
):
    atoms, chan = feat_hbm.shape
    slots = nbr_ref.shape[0]
    k_total = kidx_ref.shape[1]
    n_z = Z_HI * n_slab
    group = N_X * N_CORE
    k_loc = N_Y * n_z * EDGE
    n_dom = Z_HI * N_X * N_Y * N_CORE
    face = atoms // 8
    buf_rows = atoms + 4 * face
    nu = 1.0 / math.sqrt(atoms * n_dom * n_slab)
    mu = 1.0 / math.sqrt(k_total)

    dom = lax.axis_index("dom")
    slab = lax.axis_index("slab")
    core = lax.rem(dom, N_CORE)
    y = lax.rem(lax.div(dom, N_CORE), N_Y)
    x = lax.rem(lax.div(dom, N_CORE * N_Y), N_X)
    zh = lax.div(dom, N_CORE * N_Y * N_X)
    z = zh * n_slab + slab

    def dom_of(zh_, x_, y_, c_):
        return ((zh_ * N_X + x_) * N_Y + y_) * N_CORE + c_

    def at_xc(dx, dc):
        return (dom_of(zh, lax.rem(x + dx, N_X), y, lax.rem(core + dc, N_CORE)), slab)

    def at_y(d):
        return (dom_of(zh, x, lax.rem(y + d, N_Y), core), slab)

    def at_z(d):
        zz = lax.rem(z + d, n_z)
        return (dom_of(lax.div(zz, n_slab), x, y, core), lax.rem(zz, n_slab))

    at_dom = (
        (lax.rem(dom + n_dom - 1, n_dom), slab),
        (lax.rem(dom + 1, n_dom), slab),
        (dom, lax.rem(slab + n_slab - 1, n_slab)),
        (dom, lax.rem(slab + 1, n_slab)),
    )

    def copy(src, dst, ss, rs, dev):
        return pltpu.make_async_remote_copy(
            src_ref=src, dst_ref=dst, send_sem=ss, recv_sem=rs, device_id=dev, device_id_type=pl.DeviceIdType.MESH
        )

    xc = [(dx, dc) for dx in range(N_X) for dc in range(N_CORE)][1:]
    slot_of = {p: p[0] * N_CORE + p[1] for p in xc}
    far_first = sorted(xc, key=lambda p: -min(p[0], N_X - p[0]))
    near_first = far_first[::-1]

    peers = [at_xc(*p) for p in xc] + [at_y(d) for d in range(1, N_Y)] + [at_z(d) for d in range(1, n_z)]
    peers += [at_dom[0], at_dom[1]]
    barrier = pltpu.get_barrier_semaphore()
    for dev in peers:
        pl.semaphore_signal(barrier, inc=1, device_id=dev, device_id_type=pl.DeviceIdType.MESH)

    k_first = pl.multiple_of((dom * n_slab + slab) * EDGE, EDGE)
    results = {
        name: pltpu.make_async_copy(src, dst, st_sem.at[i])
        for i, (name, src, dst) in enumerate(
            (
                ("feat", o_feat, feat_out),
                ("pos", o_pos, pos_out),
                ("filter", o_filter, filter_out),
                ("radial", o_radial, radial_out),
                ("out", o_out, out_out),
            )
        )
    }
    loads = {}
    for i, (name, src, dst) in enumerate(
        (
            ("pos", pos_hbm, pos_ref),
            ("feat", feat_hbm, gfc.at[0, :, pl.ds(0, chan)]),
            ("cot", cot_hbm, gfc.at[0, :, pl.ds(chan, chan)]),
            ("kidx", kidx_hbm, kidx_ref),
            ("nbr", nbr_hbm, nbr_ref),
            ("cnt", cnt_hbm, cnt_ref),
            ("wrad", wrad_hbm, wrad_ref),
            ("wout", wout_hbm, wout_ref),
            ("filter", kfil_hbm.at[pl.ds(k_first, EDGE)], kf8),
        )
    ):
        loads[name] = pltpu.make_async_copy(src, dst, loc_sem.at[i])
        loads[name].start()
    m = lax.broadcasted_iota(jnp.int32, (k_loc, 1), 0)
    e = jnp.bitwise_and(m, EDGE - 1)
    place = lax.rem(lax.div(m, EDGE), n_z)
    bz = lax.rem(jnp.where(lax.rem(place, 2) == 1, lax.div(place + 1, 2), n_z - lax.div(place, 2)) + z, n_z)
    by = lax.rem(lax.div(m, EDGE * n_z) + y, N_Y)
    row = (dom_of(lax.div(bz, n_slab), x, by, core) * n_slab + lax.rem(bz, n_slab)) * EDGE + e
    column = lax.broadcasted_iota(jnp.int32, (k_loc, k_total), 1)
    picked[...] = jnp.where(row == column, 1.0, 0.0).astype(BF16)
    gpos[0] = jnp.zeros((8, atoms), F32)
    loads["pos"].wait()
    gpos[0, 0:3] = pos_ref[...]

    pl.semaphore_wait(barrier, len(peers))

    sent = []
    waits = {}

    def send(name, key, c):
        c.start()
        sent.append(c)
        waits[(name, key)] = c

    for p in far_first:
        s = slot_of[p]
        send("gp", s, copy(gpos.at[0], gpos.at[s], gp_s.at[s - 1], gp_r.at[s - 1], at_xc(*p)))
    loads["feat"].wait()
    loads["cot"].wait()
    x_order = sorted(range(1, N_X), key=lambda d: -min(d, N_X - d))
    for dx in x_order:
        s = dx * N_CORE
        send("g", s, copy(gfc.at[0], gfc.at[s], g_s.at[s - 1], g_r.at[s - 1], at_xc(dx, 0)))
    send("g", 1, copy(gfc.at[0], gfc.at[1], g_s.at[0], g_r.at[0], at_xc(0, 1)))
    for g in range(4):
        f = g ^ 1
        dev = at_dom[f]
        mine = gfc.at[0, pl.ds(f * face, face), pl.ds(0, chan)]
        send("h", g, copy(mine, hfeat.at[g], h_s.at[g], h_r.at[g], dev))
        send("hp", g, copy(gpos.at[0], hpos.at[g], hp_s.at[g], hp_r.at[g], dev))
    loads["kidx"].wait()

    pick = picked[...]
    k8 = jnp.concatenate([kidx_ref[...].astype(F32), jnp.zeros((5, k_total), F32)], axis=0)
    half = n_z * EDGE
    for d in range(N_Y):
        block = pick[d * half : (d + 1) * half]
        krow[d] = nt(k8.astype(BF16), jnp.concatenate([block, block], axis=0)).astype(BF16)
    kcol[...] = nt(pick, jnp.concatenate([k8, k8, k8, jnp.zeros_like(k8)], axis=0).astype(BF16)).astype(BF16)

    def tables(s):
        t = nn(kcol[...], split3(gpos[s]))
        cosine, sine = turns(t)
        lanes = slice(s * atoms, (s + 1) * atoms)
        both = jnp.stack([cosine.reshape(-1, EDGE, atoms), sine.reshape(-1, EDGE, atoms)], axis=1)
        csf[:, :, lanes] = both.reshape(-1, EDGE, atoms)
        csh[:, lanes] = both.reshape(-1, atoms).astype(BF16)

    tables(0)
    for p in near_first:
        s = slot_of[p]
        waits[("gp", s)].wait_recv()
        tables(s)

    def pair_setup():
        for g in range(4):
            waits[("h", g)].wait_recv()
            waits[("hp", g)].wait_recv()
        for name in ("nbr", "cnt", "wrad", "wout"):
            loads[name].wait()
        own_t = jnp.transpose(gfc[0, :, 0:chan].astype(F32))
        ghost = jnp.concatenate([hfeat[...].reshape(4 * face, chan), jnp.zeros((atoms - 4 * face, chan), BF16)], axis=0)
        ghost_t = jnp.transpose(ghost.astype(F32))
        bufft[...] = jnp.concatenate([own_t, ghost_t], axis=1).astype(BF16)
        cott[...] = jnp.transpose(gfc[0, :, chan : 2 * chan].astype(F32))
        wradt[...] = jnp.transpose(
            jnp.concatenate([wrad_ref[...].astype(F32), jnp.zeros((128 - wrad_ref.shape[0], 128), F32)], axis=0)
        ).astype(BF16)
        woutt[...] = jnp.transpose(wout_ref[...].astype(F32)).astype(BF16)
        lane = lax.broadcasted_iota(jnp.int32, (8, atoms), 1)
        ghost_pos = jnp.zeros((8, atoms), F32)
        for g in range(4):
            moved = pltpu.roll(hpos[g], (face if g % 2 else atoms - face), axis=1)
            ghost_pos = jnp.where((lane >= g * face) & (lane < (g + 1) * face), moved, ghost_pos)
        possp[:, 0:atoms] = split3(gpos[0])
        possp[:, atoms : 2 * atoms] = split3(ghost_pos)
        for ref in (dbf, dbp, ownp, pwo, pwr):
            ref[...] = jnp.zeros(ref.shape, F32)

    levels = wrad_ref.shape[0]
    rates = 0.5 * jnp.exp(
        lax.broadcasted_iota(jnp.int32, (levels, 1), 0).astype(F32) * (math.log(16.0) / (levels - 1))
    )

    span = 2
    width = span * atoms

    def weights(first):
        return jnp.concatenate(
            [cott[...] * jnp.where(cnt_ref[...] > first + j, slots**-0.5, 0.0) for j in range(span)], axis=1
        )

    def pair_first(q):
        first = q * span
        here = slice(q * width, (q + 1) * width)
        idx = jnp.concatenate([nbr_ref[first + j : first + j + 1, :] for j in range(span)], axis=1)
        hot = jnp.where(lax.broadcasted_iota(jnp.int32, (buf_rows, width), 0) == idx, 1.0, 0.0).astype(BF16)
        tp = nn(possp[:, 0:buf_rows], hot)
        target = tp[0:8] + tp[8:16] + tp[16:24]
        source = jnp.concatenate([gpos[0]] * span, axis=1)
        cosine, chord = turns(target - source)
        dist2 = jnp.sum(chord * chord, axis=0, keepdims=True)
        rbf = jnp.exp(-rates * dist2)
        rbf_h = rbf.astype(BF16)
        pre = nn(wradt[:, 0:levels], rbf_h)
        gate = 0.5 * jnp.tanh(0.5 * pre) + 0.5
        act = (pre * gate).astype(BF16)
        dphi = (weights(first) * nn(bufft[:, 0:buf_rows], hot)).astype(BF16)
        pwo[...] += nt(act, dphi)
        d_act = nn(wout_ref[...], dphi)
        dpre = (d_act * gate * (1.0 + pre * (1.0 - gate))).astype(BF16)
        pwr[...] += nt(rbf_h, dpre)
        hot_s[:, here] = hot
        act_s[:, here] = act
        dpre_s[:, here] = dpre
        rbf_s[:, here] = rbf
        chord_s[:, here] = chord
        cosine_s[:, here] = cosine

    def pair_second(q):
        here = slice(q * width, (q + 1) * width)
        hot = hot_s[:, here]
        given = weights(q * span) * nn(woutt[...], act_s[:, here])
        given_hi = given.astype(BF16)
        given_lo = (given - given_hi.astype(F32)).astype(BF16)
        added = nt(hot, jnp.concatenate([given_hi, given_lo], axis=0))
        dbf[...] += added[:, 0:chan] + added[:, chan : 2 * chan]
        d_rbf = nn(wrad_ref[...], dpre_s[:, here])
        d_chord2 = -jnp.sum(d_rbf * rates * rbf_s[:, here], axis=0, keepdims=True)
        dmove = (2.0 * mu) * d_chord2 * chord_s[:, here] * cosine_s[:, here]
        move_hi = dmove.astype(BF16).astype(F32)
        moves = nt(jnp.concatenate([move_hi, dmove - move_hi], axis=0).astype(BF16), hot)
        dbp[...] += moves[0:8] + moves[8:16]
        for j in range(span):
            ownp[...] -= dmove[:, j * atoms : (j + 1) * atoms]

    out_rows = pwo.shape[0] // group
    rad_rows = levels // group
    my_piece = x * N_CORE + core

    def pair_sends():
        for j in range(group):
            pw_a[j, 0:out_rows] = pwo[j * out_rows : (j + 1) * out_rows, :]
            tail = pwr[j * rad_rows : (j + 1) * rad_rows, :]
            pw_a[j, out_rows:] = jnp.concatenate([tail, jnp.zeros((8 - rad_rows, tail.shape[1]), F32)], axis=0)
        for p in far_first:
            s = slot_of[p]
            piece = lax.rem(x + p[0], N_X) * N_CORE + lax.rem(core + p[1], N_CORE)
            send("pa", s, copy(pw_a.at[piece], pw_ar.at[s - 1], pa_s.at[s - 1], pa_r.at[s - 1], at_xc(*p)))

    def hand_over(dx):
        s = dx * N_CORE
        waits[("g", s)].wait_recv()
        send("g", s + 1, copy(gfc.at[s], gfc.at[s + 1], g_s.at[s], g_r.at[s], at_xc(0, 1)))

    def chip_part(dx, rows):
        lanes = slice(dx * N_CORE * atoms, (dx + 1) * N_CORE * atoms)
        return nn(csh[rows, lanes], gfc[dx * N_CORE : (dx + 1) * N_CORE].reshape(N_CORE * atoms, 2 * chan))

    dz_at = [(p + 1) // 2 if p % 2 else (n_z - p // 2) % n_z for p in range(n_z)]
    place_of = {dz: p for p, dz in enumerate(dz_at)}
    z_rows = 2 * EDGE
    near_z = n_z * NEAR // 8
    parts = ((near_z, n_z), (0, near_z))
    y_rows = n_z * 2 * EDGE
    near_x = x_order[::-1]
    all_rows = slice(0, 2 * k_loc)
    chunks = slots // 2
    for dx in near_x[:-1]:
        hand_over(dx)
    waits[("g", 1)].wait_recv()
    pacc[...] = chip_part(0, all_rows)
    hand_over(near_x[-1])
    for dx in near_x[:-1]:
        waits[("g", dx * N_CORE + 1)].wait_recv()
        pacc[...] += chip_part(dx, all_rows)
    waits[("g", near_x[-1] * N_CORE + 1)].wait_recv()
    y_order = sorted(range(1, N_Y), key=lambda d: -min(d, N_Y - d))

    def send_y(g, d):
        rows = pl.ds(parts[g][0] * z_rows, (parts[g][1] - parts[g][0]) * z_rows)
        i = 2 * d - 2 + g
        send("y", (g, d), copy(ysend.at[d - 1, rows], yrecv.at[d - 1, rows], y_s.at[i], y_r.at[i], at_y(d)))

    for d in y_order + [0]:
        rows = slice(d * y_rows, (d + 1) * y_rows)
        part = pacc[rows, :] + chip_part(near_x[-1], rows)
        if d:
            ysend[d - 1] = part.astype(BF16)
            send_y(0, d)
        else:
            yown[...] = part
    for d in y_order:
        send_y(1, d)

    first_part = chunks * PART // 8
    pair_setup()
    for q in range(first_part):
        pair_first(q)
    if first_part == chunks:
        pair_sends()

    for g, (lo, hi) in enumerate(parts):
        rows = slice(lo * z_rows, hi * z_rows)
        total = yown[rows, :]
        for d in range(1, N_Y):
            waits[("y", (g, d))].wait_recv()
            total = total + yrecv[d - 1, rows].astype(F32)
        for p in range(hi - 1, lo - 1, -1):
            block = total[(p - lo) * z_rows : (p - lo + 1) * z_rows, :]
            d = dz_at[p]
            if d:
                zsend[d - 1] = block.astype(BF16)
                send("z", d, copy(zsend.at[d - 1], zrecv.at[d - 1], z_s.at[d - 1], z_r.at[d - 1], at_z(d)))
            else:
                mine = block
    for q in range(first_part, chunks):
        pair_first(q)
    if first_part < chunks:
        pair_sends()

    for s in range(group):
        gfct[:, s * atoms : (s + 1) * atoms] = jnp.transpose(gfc[s].astype(F32)).astype(BF16)

    for d in range(1, n_z):
        waits[("z", d)].wait_recv()
        mine = mine + zrecv[d - 1].astype(F32)
    mine = nu * mine
    loads["filter"].wait()
    kf = jnp.concatenate([kf8[...], kf8[...]], axis=0)
    wbuf[0, 0] = jnp.concatenate([kf * mine[:, chan : 2 * chan], kf * mine[:, 0:chan]], axis=1).astype(BF16)
    z_order = dz_at[:0:-1]
    for d in z_order:
        there = n_z - d
        to = wbuf.at[0, place_of[there]]
        send("za", there, copy(wbuf.at[0, 0], to, za_s.at[d - 1], za_r.at[there - 1], at_z(d)))
    o_filter[...] = (
        mine[0:EDGE, 0:chan] * mine[0:EDGE, chan : 2 * chan]
        + mine[EDGE : 2 * EDGE, 0:chan] * mine[EDGE : 2 * EDGE, chan : 2 * chan]
    )
    results["filter"].start()

    for q in range(chunks):
        pair_second(q)
    dgp[...] = jnp.concatenate([dbp[:, atoms:buf_rows], jnp.zeros((8, 2 * atoms - buf_rows), F32)], axis=1)
    for g in range(4):
        send("rf", g, copy(dbf.at[pl.ds(atoms + g * face, face)], retf.at[g], rf_s.at[g], rf_r.at[g], at_dom[g]))
        send("rp", g, copy(dgp, retp.at[g], rp_s.at[g], rp_r.at[g], at_dom[g]))

    for p in xc:
        waits[("pa", slot_of[p])].wait_recv()
    piece_sum = pw_a[my_piece]
    for s in range(group - 1):
        piece_sum = piece_sum + pw_ar[s]
    pw_b[...] = piece_sum
    for d in z_order:
        send("pb", d, copy(pw_b, pw_br.at[d - 1], pb_s.at[d - 1], pb_r.at[d - 1], at_z(d)))

    for g in (1, 0):
        lo, hi = parts[g]
        for p in range(max(lo, 1), hi):
            waits[("za", dz_at[p])].wait_recv()
        for d in y_order:
            there = N_Y - d
            i = 2 * there - 2 + g
            blocks = pl.ds(lo, hi - lo)
            to = wbuf.at[there, blocks]
            send("ya", (g, there), copy(wbuf.at[0, blocks], to, ya_s.at[2 * d - 2 + g], ya_r.at[i], at_y(d)))

    for d in range(1, n_z):
        waits[("pb", d)].wait_recv()
        piece_sum = piece_sum + pw_br[d - 1]
    pw_c[...] = piece_sum
    for d in y_order:
        send("pc", d, copy(pw_c, pw_cr.at[d - 1], pc_s.at[d - 1], pc_r.at[d - 1], at_y(d)))

    for g in range(4):
        waits[("rf", g)].wait_recv()
        waits[("rp", g)].wait_recv()
    lane = lax.broadcasted_iota(jnp.int32, (8, atoms), 1)
    short_pos = dbp[:, 0:atoms] + ownp[...]
    for g in range(4):
        f = g ^ 1
        moved = pltpu.roll(retp[g], (atoms - face if g % 2 else face), axis=1)
        short_pos = short_pos + jnp.where((lane >= f * face) & (lane < (f + 1) * face), moved, 0.0)
        rows = slice(f * face, (f + 1) * face)
        dbf[rows, :] += retf[g]
    ownp[...] = short_pos

    def turned(d):
        return jnp.transpose(wbuf[d].reshape(y_rows, 2 * chan)[:, 0:chan].astype(F32)).astype(BF16)

    def give_back(d, fg_t, first, count):
        lanes = slice(first * atoms, (first + count) * atoms)
        rows = slice(d * y_rows, (d + 1) * y_rows)
        w = wbuf[d].reshape(y_rows, 2 * chan)
        d_feat_t = nn(fg_t, csh[rows, lanes])
        pq = nn(w, gfct[:, lanes]).reshape(-1, 2, EDGE, count * atoms)
        cs = csf[d * y_rows // EDGE : (d + 1) * y_rows // EDGE, :, lanes].reshape(-1, 2, EDGE, count * atoms)
        wave = (cs[:, 0] * pq[:, 1] - cs[:, 1] * pq[:, 0]).reshape(half, count * atoms)
        hi = wave.astype(BF16).astype(F32)
        d_pos = mu * nn(krow[d], jnp.concatenate([hi, wave - hi], axis=0).astype(BF16))
        return d_feat_t, d_pos

    for d in [0] + y_order[::-1][:-1]:
        if d:
            waits[("ya", (1, d))].wait_recv()
            waits[("ya", (0, d))].wait_recv()
        fg_t = turned(d)
        for first in range(0, group, 2):
            lanes = slice(first * atoms, (first + 2) * atoms)
            d_feat_t, d_pos = give_back(d, fg_t, first, 2)
            if d:
                facc[:, lanes] += d_feat_t
                xacc[:, lanes] += d_pos
            else:
                facc[:, lanes] = d_feat_t
                xacc[:, lanes] = d_pos
    last = y_order[0]
    waits[("ya", (1, last))].wait_recv()
    waits[("ya", (0, last))].wait_recv()
    fg_last = turned(last)

    for d in range(1, N_Y):
        waits[("pc", d)].wait_recv()
        piece_sum = piece_sum + pw_cr[d - 1]
    pw_d[my_piece] = nu * piece_sum
    for p in far_first:
        s = slot_of[p]
        send("pd", s, copy(pw_d.at[my_piece], pw_d.at[my_piece], pd_s.at[s - 1], pd_r.at[s - 1], at_xc(*p)))

    def whole(s):
        lanes = slice(s * atoms, (s + 1) * atoms)
        d_feat_t, d_pos = give_back(last, fg_last, s, 1)
        return facc[:, lanes] + d_feat_t, xacc[:, lanes] + d_pos

    for dx in x_order + [0]:
        d_feat_t, d_pos = whole(dx * N_CORE + 1)
        outs_c[dx, 0:chan] = d_feat_t
        outs_c[dx, chan:] = d_pos
        send("oc", dx, copy(outs_c.at[dx], outr_c.at[dx], oc_s.at[dx], oc_r.at[dx], at_xc(0, 1)))
    for dx in x_order:
        d_feat_t, d_pos = whole(dx * N_CORE)
        waits[("oc", dx)].wait_recv()
        d_feat_t = d_feat_t + outr_c[dx, 0:chan]
        d_pos = d_pos + outr_c[dx, chan:]
        pos_hi = d_pos.astype(BF16).astype(F32)
        outs_x[dx - 1] = jnp.concatenate([d_feat_t, pos_hi, d_pos - pos_hi], axis=0).astype(BF16)
        send("ox", dx, copy(outs_x.at[dx - 1], outr_x.at[dx - 1], ox_s.at[dx - 1], ox_r.at[dx - 1], at_xc(N_X - dx, 0)))

    long_t, long_pos = whole(0)
    waits[("oc", 0)].wait_recv()
    long_t = long_t + outr_c[0, 0:chan]
    long_pos = long_pos + outr_c[0, chan:]
    for dx in near_x:
        waits[("ox", dx)].wait_recv()
        got = outr_x[dx - 1].astype(F32)
        long_t = long_t + got[0:chan]
        long_pos = long_pos + got[chan : chan + 8] + got[chan + 8 : chan + 16]
    o_feat[...] = jnp.transpose(long_t) + dbf[0:atoms, :]
    o_pos[...] = (long_pos + ownp[...])[0:3]
    results["feat"].start()
    results["pos"].start()

    for p in xc:
        waits[("pd", slot_of[p])].wait_recv()
    for j in range(group):
        o_out[j * out_rows : (j + 1) * out_rows, :] = pw_d[j, 0:out_rows]
        o_radial[j * rad_rows : (j + 1) * rad_rows, :] = pw_d[j, out_rows : out_rows + rad_rows]
    results["out"].start()
    results["radial"].start()
    for c in sent:
        c.wait_send()
    for c in results.values():
        c.wait()


def store(*refs):
    n = len(refs) // 2
    for src, dst in zip(refs[:n], refs[n:]):
        dst[...] = src[...]


def shards(features, cotangent, positions, neighbours, counts, k_index, k_filter, w_radial, w_out):
    n_slab = lax.axis_size("slab")
    atoms, chan = features.shape
    levels, hidden = w_radial.shape
    group = N_X * N_CORE
    n_z = Z_HI * n_slab
    k_loc = N_Y * n_z * EDGE
    face = atoms // 8
    buf_rows = atoms + 4 * face
    piece = hidden // group + 8
    pairs = atoms * neighbours.shape[0]
    v = pltpu.VMEM
    dma = pltpu.SemaphoreType.DMA
    scratch = [
        v((atoms, chan), F32),
        v((3, atoms), F32),
        v((EDGE, chan), F32),
        v((levels, hidden), F32),
        v((hidden, chan), F32),
        v(positions.shape, F32),
        v(neighbours.shape, jnp.int32),
        v((1, atoms), jnp.int32),
        v(k_index.shape, jnp.int32),
        v(w_radial.shape, BF16),
        v(w_out.shape, BF16),
        v((group, atoms, 2 * chan), BF16),
        v((group, 8, atoms), F32),
        v((4, face, chan), BF16),
        v((4, 8, atoms), F32),
        v((2 * k_loc // EDGE, EDGE, group * atoms), F32),
        v((2 * k_loc, group * atoms), BF16),
        v((N_Y - 1, 2 * n_z * EDGE, 2 * chan), BF16),
        v((2 * n_z * EDGE, 2 * chan), F32),
        v((N_Y - 1, 2 * n_z * EDGE, 2 * chan), BF16),
        v((n_z - 1, 2 * EDGE, 2 * chan), BF16),
        v((n_z - 1, 2 * EDGE, 2 * chan), BF16),
        v((N_Y, n_z, 2 * EDGE, 2 * chan), BF16),
        v((EDGE, chan), F32),
        v((k_loc, k_index.shape[1]), BF16),
        v((2 * chan, group * atoms), BF16),
        v((buf_rows, pairs), BF16),
        v((hidden, pairs), BF16),
        v((hidden, pairs), BF16),
        v((levels, pairs), F32),
        v((8, pairs), F32),
        v((8, pairs), F32),
        v((2 * k_loc, 2 * chan), F32),
        v((chan, group * atoms), F32),
        v((8, group * atoms), F32),
        v((N_X, chan + 8, atoms), F32),
        v((N_X, chan + 8, atoms), F32),
        v((N_X - 1, chan + 16, atoms), BF16),
        v((N_X - 1, chan + 16, atoms), BF16),
        v((k_loc, 32), BF16),
        v((N_Y, 8, 2 * n_z * EDGE), BF16),
        v((chan, 2 * atoms), BF16),
        v((32, 2 * atoms), BF16),
        v((chan, atoms), F32),
        v((hidden, 128), BF16),
        v((chan, hidden), BF16),
        v((buf_rows, chan), F32),
        v((8, buf_rows), F32),
        v((8, atoms), F32),
        v((8, atoms), F32),
        v((hidden, chan), F32),
        v((levels, hidden), F32),
        v((4, face, chan), F32),
        v((4, 8, atoms), F32),
        v((group, piece, chan), F32),
        v((group - 1, piece, chan), F32),
        v((piece, chan), F32),
        v((n_z - 1, piece, chan), F32),
        v((piece, chan), F32),
        v((N_Y - 1, piece, chan), F32),
        v((group, piece, chan), F32),
        dma((9,)),
        dma((5,)),
    ]
    for n in (group - 1, group - 1, 4, 4, 2 * N_Y - 2, n_z - 1, n_z - 1, 2 * N_Y - 2):
        scratch += [dma((n,)), dma((n,))]
    for n in (N_X, N_X - 1, 4, 4, group - 1, n_z - 1, N_Y - 1, group - 1):
        scratch += [dma((n,)), dma((n,))]
    hbm = pl.BlockSpec(memory_space=pltpu.HBM)
    vmem = pl.BlockSpec(memory_space=pltpu.VMEM)
    shapes = (
        jax.ShapeDtypeStruct((atoms, chan), F32),
        jax.ShapeDtypeStruct((3, atoms), F32),
        jax.ShapeDtypeStruct((EDGE, chan), F32),
        jax.ShapeDtypeStruct((levels, hidden), F32),
        jax.ShapeDtypeStruct((hidden, chan), F32),
    )
    results = pl.pallas_call(
        functools.partial(body, n_slab),
        out_shape=shapes,
        in_specs=[hbm] * 9,
        out_specs=(hbm,) * 5,
        scratch_shapes=scratch,
        compiler_params=pltpu.CompilerParams(
            collective_id=0, has_side_effects=True, vmem_limit_bytes=56 << 20
        ),
        name="ewald",
    )(
        features,
        cotangent,
        positions,
        neighbours,
        counts.reshape(1, atoms),
        k_index,
        k_filter,
        w_radial,
        w_out,
    )
    return pl.pallas_call(
        store,
        out_shape=shapes,
        in_specs=[vmem] * 5,
        out_specs=(vmem,) * 5,
        compiler_params=pltpu.CompilerParams(vmem_limit_bytes=56 << 20),
        name="store",
    )(*results)


def solution(mesh):
    both = ("dom", "slab")
    in_specs = (P(both, None), P(both, None), P(None, both), P(None, both), P(both), P(), P(), P(), P())
    out_specs = (P(both, None), P(None, both), P(both, None), P(), P())
    return jax.shard_map(shards, mesh=mesh, in_specs=in_specs, out_specs=out_specs, check_vma=False)
```

```python
import functools
import math

import jax
import jax.numpy as jnp
from jax import lax
from jax.experimental import pallas as pl
from jax.experimental.pallas import tpu as pltpu
from jax.sharding import PartitionSpec as P

Z_HI, N_X, N_Y, N_CORE = 2, 4, 4, 2
EDGE = 8
PART = 6
NEAR = 5
F32 = jnp.float32
BF16 = jnp.bfloat16

SIN_C = (3.1415926401307077, -5.167710083507896, 2.550077523214726, -0.5982912856213906, 0.07765766030763246)
COS_C = (
    0.9999999997799044,
    -4.934802137078806,
    4.058709159555702,
    -1.3352120030438075,
    0.23493731378604543,
    -0.024396324301093893,
)


def horner(coefs, u):
    y = coefs[-1] * u + coefs[-2]
    for k in coefs[-3::-1]:
        y = y * u + k
    return y


def turns(t):
    r = t - jnp.round(t)
    u = r * r
    s = r * horner(SIN_C, u)
    c = horner(COS_C, u)
    return 1.0 - 2.0 * (s * s), 2.0 * (s * c)


def split3(v):
    hi = v.astype(BF16)
    rest = v - hi.astype(F32)
    mid = rest.astype(BF16)
    lo = (rest - mid.astype(F32)).astype(BF16)
    return jnp.concatenate([hi.astype(F32), mid.astype(F32), lo.astype(F32), jnp.zeros_like(v)], axis=0).astype(BF16)


def nn(a, b):
    return lax.dot_general(a, b, (((1,), (0,)), ((), ())), preferred_element_type=F32)


def nt(a, b):
    return lax.dot_general(a, b, (((1,), (1,)), ((), ())), preferred_element_type=F32)


def body(
    n_slab,
    feat_hbm,
    cot_hbm,
    pos_hbm,
    nbr_hbm,
    cnt_hbm,
    kidx_hbm,
    kfil_hbm,
    wrad_hbm,
    wout_hbm,
    o_feat,
    o_pos,
    o_filter,
    o_radial,
    o_out,
    pos_ref,
    nbr_ref,
    cnt_ref,
    kidx_ref,
    wrad_ref,
    wout_ref,
    gfc,
    gpos,
    hfeat,
    hpos,
    csf,
    csh,
    ysend,
    yown,
    yrecv,
    zsend,
    zrecv,
    wbuf,
    kf8,
    picked,
    gfct,
    hot_s,
    act_s,
    dpre_s,
    rbf_s,
    chord_s,
    cosine_s,
    pacc,
    facc,
    xacc,
    outs_c,
    outr_c,
    outs_x,
    outr_x,
    kcol,
    krow,
    bufft,
    possp,
    cott,
    wradt,
    woutt,
    dbf,
    dbp,
    dgp,
    ownp,
    pwo,
    pwr,
    retf,
    retp,
    pw_a,
    pw_ar,
    pw_b,
    pw_br,
    pw_c,
    pw_cr,
    pw_d,
    loc_sem,
    g_s,
    g_r,
    gp_s,
    gp_r,
    h_s,
    h_r,
    hp_s,
    hp_r,
    y_s,
    y_r,
    z_s,
    z_r,
    za_s,
    za_r,
    ya_s,
    ya_r,
    oc_s,
    oc_r,
    ox_s,
    ox_r,
    rf_s,
    rf_r,
    rp_s,
    rp_r,
    pa_s,
    pa_r,
    pb_s,
    pb_r,
    pc_s,
    pc_r,
    pd_s,
    pd_r,
):
    atoms, chan = feat_hbm.shape
    slots = nbr_ref.shape[0]
    k_total = kidx_ref.shape[1]
    n_z = Z_HI * n_slab
    group = N_X * N_CORE
    k_loc = N_Y * n_z * EDGE
    n_dom = Z_HI * N_X * N_Y * N_CORE
    face = atoms // 8
    buf_rows = atoms + 4 * face
    nu = 1.0 / math.sqrt(atoms * n_dom * n_slab)
    mu = 1.0 / math.sqrt(k_total)

    dom = lax.axis_index("dom")
    slab = lax.axis_index("slab")
    core = lax.rem(dom, N_CORE)
    y = lax.rem(lax.div(dom, N_CORE), N_Y)
    x = lax.rem(lax.div(dom, N_CORE * N_Y), N_X)
    zh = lax.div(dom, N_CORE * N_Y * N_X)
    z = zh * n_slab + slab

    def dom_of(zh_, x_, y_, c_):
        return ((zh_ * N_X + x_) * N_Y + y_) * N_CORE + c_

    def at_xc(dx, dc):
        return (dom_of(zh, lax.rem(x + dx, N_X), y, lax.rem(core + dc, N_CORE)), slab)

    def at_y(d):
        return (dom_of(zh, x, lax.rem(y + d, N_Y), core), slab)

    def at_z(d):
        zz = lax.rem(z + d, n_z)
        return (dom_of(lax.div(zz, n_slab), x, y, core), lax.rem(zz, n_slab))

    at_dom = (
        (lax.rem(dom + n_dom - 1, n_dom), slab),
        (lax.rem(dom + 1, n_dom), slab),
        (dom, lax.rem(slab + n_slab - 1, n_slab)),
        (dom, lax.rem(slab + 1, n_slab)),
    )

    def copy(src, dst, ss, rs, dev):
        return pltpu.make_async_remote_copy(
            src_ref=src, dst_ref=dst, send_sem=ss, recv_sem=rs, device_id=dev, device_id_type=pl.DeviceIdType.MESH
        )

    xc = [(dx, dc) for dx in range(N_X) for dc in range(N_CORE)][1:]
    slot_of = {p: p[0] * N_CORE + p[1] for p in xc}
    far_first = sorted(xc, key=lambda p: -min(p[0], N_X - p[0]))
    near_first = far_first[::-1]

    peers = [at_xc(*p) for p in xc] + [at_y(d) for d in range(1, N_Y)] + [at_z(d) for d in range(1, n_z)]
    peers += [at_dom[0], at_dom[1]]
    barrier = pltpu.get_barrier_semaphore()
    for dev in peers:
        pl.semaphore_signal(barrier, inc=1, device_id=dev, device_id_type=pl.DeviceIdType.MESH)

    k_first = pl.multiple_of((dom * n_slab + slab) * EDGE, EDGE)
    loads = {}
    for i, (name, src, dst) in enumerate(
        (
            ("pos", pos_hbm, pos_ref),
            ("feat", feat_hbm, gfc.at[0, :, pl.ds(0, chan)]),
            ("cot", cot_hbm, gfc.at[0, :, pl.ds(chan, chan)]),
            ("kidx", kidx_hbm, kidx_ref),
            ("nbr", nbr_hbm, nbr_ref),
            ("cnt", cnt_hbm, cnt_ref),
            ("wrad", wrad_hbm, wrad_ref),
            ("wout", wout_hbm, wout_ref),
            ("filter", kfil_hbm.at[pl.ds(k_first, EDGE)], kf8),
        )
    ):
        loads[name] = pltpu.make_async_copy(src, dst, loc_sem.at[i])
        loads[name].start()
    m = lax.broadcasted_iota(jnp.int32, (k_loc, 1), 0)
    e = jnp.bitwise_and(m, EDGE - 1)
    place = lax.rem(lax.div(m, EDGE), n_z)
    bz = lax.rem(jnp.where(lax.rem(place, 2) == 1, lax.div(place + 1, 2), n_z - lax.div(place, 2)) + z, n_z)
    by = lax.rem(lax.div(m, EDGE * n_z) + y, N_Y)
    row = (dom_of(lax.div(bz, n_slab), x, by, core) * n_slab + lax.rem(bz, n_slab)) * EDGE + e
    column = lax.broadcasted_iota(jnp.int32, (k_loc, k_total), 1)
    picked[...] = jnp.where(row == column, 1.0, 0.0).astype(BF16)
    gpos[0] = jnp.zeros((8, atoms), F32)
    loads["pos"].wait()
    gpos[0, 0:3] = pos_ref[...]

    pl.semaphore_wait(barrier, len(peers))

    sent = []
    waits = {}

    def send(name, key, c):
        c.start()
        sent.append(c)
        waits[(name, key)] = c

    for p in far_first:
        s = slot_of[p]
        send("gp", s, copy(gpos.at[0], gpos.at[s], gp_s.at[s - 1], gp_r.at[s - 1], at_xc(*p)))
    loads["feat"].wait()
    loads["cot"].wait()
    x_order = sorted(range(1, N_X), key=lambda d: -min(d, N_X - d))
    for dx in x_order:
        s = dx * N_CORE
        send("g", s, copy(gfc.at[0], gfc.at[s], g_s.at[s - 1], g_r.at[s - 1], at_xc(dx, 0)))
    send("g", 1, copy(gfc.at[0], gfc.at[1], g_s.at[0], g_r.at[0], at_xc(0, 1)))
    for g in range(4):
        f = g ^ 1
        dev = at_dom[f]
        mine = gfc.at[0, pl.ds(f * face, face), pl.ds(0, chan)]
        send("h", g, copy(mine, hfeat.at[g], h_s.at[g], h_r.at[g], dev))
        send("hp", g, copy(gpos.at[0], hpos.at[g], hp_s.at[g], hp_r.at[g], dev))
    loads["kidx"].wait()

    pick = picked[...]
    k8 = jnp.concatenate([kidx_ref[...].astype(F32), jnp.zeros((5, k_total), F32)], axis=0)
    half = n_z * EDGE
    for d in range(N_Y):
        block = pick[d * half : (d + 1) * half]
        krow[d] = nt(k8.astype(BF16), jnp.concatenate([block, block], axis=0)).astype(BF16)
    kcol[...] = nt(pick, jnp.concatenate([k8, k8, k8, jnp.zeros_like(k8)], axis=0).astype(BF16)).astype(BF16)

    def tables(s):
        t = nn(kcol[...], split3(gpos[s]))
        cosine, sine = turns(t)
        lanes = slice(s * atoms, (s + 1) * atoms)
        both = jnp.stack([cosine.reshape(-1, EDGE, atoms), sine.reshape(-1, EDGE, atoms)], axis=1)
        csf[:, :, lanes] = both.reshape(-1, EDGE, atoms)
        csh[:, lanes] = both.reshape(-1, atoms).astype(BF16)

    tables(0)
    for p in near_first:
        s = slot_of[p]
        waits[("gp", s)].wait_recv()
        tables(s)

    def pair_setup():
        for g in range(4):
            waits[("h", g)].wait_recv()
            waits[("hp", g)].wait_recv()
        for name in ("nbr", "cnt", "wrad", "wout"):
            loads[name].wait()
        own_t = jnp.transpose(gfc[0, :, 0:chan].astype(F32))
        ghost = jnp.concatenate([hfeat[...].reshape(4 * face, chan), jnp.zeros((atoms - 4 * face, chan), BF16)], axis=0)
        ghost_t = jnp.transpose(ghost.astype(F32))
        bufft[...] = jnp.concatenate([own_t, ghost_t], axis=1).astype(BF16)
        cott[...] = jnp.transpose(gfc[0, :, chan : 2 * chan].astype(F32))
        wradt[...] = jnp.transpose(
            jnp.concatenate([wrad_ref[...].astype(F32), jnp.zeros((128 - wrad_ref.shape[0], 128), F32)], axis=0)
        ).astype(BF16)
        woutt[...] = jnp.transpose(wout_ref[...].astype(F32)).astype(BF16)
        lane = lax.broadcasted_iota(jnp.int32, (8, atoms), 1)
        ghost_pos = jnp.zeros((8, atoms), F32)
        for g in range(4):
            moved = pltpu.roll(hpos[g], (face if g % 2 else atoms - face), axis=1)
            ghost_pos = jnp.where((lane >= g * face) & (lane < (g + 1) * face), moved, ghost_pos)
        possp[:, 0:atoms] = split3(gpos[0])
        possp[:, atoms : 2 * atoms] = split3(ghost_pos)
        for ref in (dbf, dbp, ownp, pwo, pwr):
            ref[...] = jnp.zeros(ref.shape, F32)

    levels = wrad_ref.shape[0]
    rates = 0.5 * jnp.exp(
        lax.broadcasted_iota(jnp.int32, (levels, 1), 0).astype(F32) * (math.log(16.0) / (levels - 1))
    )

    span = 2
    width = span * atoms

    def weights(first):
        return jnp.concatenate(
            [cott[...] * jnp.where(cnt_ref[...] > first + j, slots**-0.5, 0.0) for j in range(span)], axis=1
        )

    def pair_first(q):
        first = q * span
        here = slice(q * width, (q + 1) * width)
        idx = jnp.concatenate([nbr_ref[first + j : first + j + 1, :] for j in range(span)], axis=1)
        hot = jnp.where(lax.broadcasted_iota(jnp.int32, (buf_rows, width), 0) == idx, 1.0, 0.0).astype(BF16)
        tp = nn(possp[:, 0:buf_rows], hot)
        target = tp[0:8] + tp[8:16] + tp[16:24]
        source = jnp.concatenate([gpos[0]] * span, axis=1)
        cosine, chord = turns(target - source)
        dist2 = jnp.sum(chord * chord, axis=0, keepdims=True)
        rbf = jnp.exp(-rates * dist2)
        rbf_h = rbf.astype(BF16)
        pre = nn(wradt[:, 0:levels], rbf_h)
        gate = 0.5 * jnp.tanh(0.5 * pre) + 0.5
        act = (pre * gate).astype(BF16)
        dphi = (weights(first) * nn(bufft[:, 0:buf_rows], hot)).astype(BF16)
        pwo[...] += nt(act, dphi)
        d_act = nn(wout_ref[...], dphi)
        dpre = (d_act * gate * (1.0 + pre * (1.0 - gate))).astype(BF16)
        pwr[...] += nt(rbf_h, dpre)
        hot_s[:, here] = hot
        act_s[:, here] = act
        dpre_s[:, here] = dpre
        rbf_s[:, here] = rbf
        chord_s[:, here] = chord
        cosine_s[:, here] = cosine

    def pair_second(q):
        here = slice(q * width, (q + 1) * width)
        hot = hot_s[:, here]
        given = weights(q * span) * nn(woutt[...], act_s[:, here])
        given_hi = given.astype(BF16)
        given_lo = (given - given_hi.astype(F32)).astype(BF16)
        added = nt(hot, jnp.concatenate([given_hi, given_lo], axis=0))
        dbf[...] += added[:, 0:chan] + added[:, chan : 2 * chan]
        d_rbf = nn(wrad_ref[...], dpre_s[:, here])
        d_chord2 = -jnp.sum(d_rbf * rates * rbf_s[:, here], axis=0, keepdims=True)
        dmove = (2.0 * mu) * d_chord2 * chord_s[:, here] * cosine_s[:, here]
        move_hi = dmove.astype(BF16).astype(F32)
        moves = nt(jnp.concatenate([move_hi, dmove - move_hi], axis=0).astype(BF16), hot)
        dbp[...] += moves[0:8] + moves[8:16]
        for j in range(span):
            ownp[...] -= dmove[:, j * atoms : (j + 1) * atoms]

    out_rows = pwo.shape[0] // group
    rad_rows = levels // group
    my_piece = x * N_CORE + core

    def pair_sends():
        for j in range(group):
            pw_a[j, 0:out_rows] = pwo[j * out_rows : (j + 1) * out_rows, :]
            tail = pwr[j * rad_rows : (j + 1) * rad_rows, :]
            pw_a[j, out_rows:] = jnp.concatenate([tail, jnp.zeros((8 - rad_rows, tail.shape[1]), F32)], axis=0)
        for p in far_first:
            s = slot_of[p]
            piece = lax.rem(x + p[0], N_X) * N_CORE + lax.rem(core + p[1], N_CORE)
            send("pa", s, copy(pw_a.at[piece], pw_ar.at[s - 1], pa_s.at[s - 1], pa_r.at[s - 1], at_xc(*p)))

    def hand_over(dx):
        s = dx * N_CORE
        waits[("g", s)].wait_recv()
        send("g", s + 1, copy(gfc.at[s], gfc.at[s + 1], g_s.at[s], g_r.at[s], at_xc(0, 1)))

    def chip_part(dx, rows):
        lanes = slice(dx * N_CORE * atoms, (dx + 1) * N_CORE * atoms)
        return nn(csh[rows, lanes], gfc[dx * N_CORE : (dx + 1) * N_CORE].reshape(N_CORE * atoms, 2 * chan))

    dz_at = [(p + 1) // 2 if p % 2 else (n_z - p // 2) % n_z for p in range(n_z)]
    place_of = {dz: p for p, dz in enumerate(dz_at)}
    z_rows = 2 * EDGE
    near_z = n_z * NEAR // 8
    parts = ((near_z, n_z), (0, near_z))
    y_rows = n_z * 2 * EDGE
    near_x = x_order[::-1]
    all_rows = slice(0, 2 * k_loc)
    chunks = slots // 2
    for dx in near_x[:-1]:
        hand_over(dx)
    waits[("g", 1)].wait_recv()
    pacc[...] = chip_part(0, all_rows)
    hand_over(near_x[-1])
    for dx in near_x[:-1]:
        waits[("g", dx * N_CORE + 1)].wait_recv()
        pacc[...] += chip_part(dx, all_rows)
    waits[("g", near_x[-1] * N_CORE + 1)].wait_recv()
    y_order = sorted(range(1, N_Y), key=lambda d: -min(d, N_Y - d))

    def send_y(g, d):
        rows = pl.ds(parts[g][0] * z_rows, (parts[g][1] - parts[g][0]) * z_rows)
        i = 2 * d - 2 + g
        send("y", (g, d), copy(ysend.at[d - 1, rows], yrecv.at[d - 1, rows], y_s.at[i], y_r.at[i], at_y(d)))

    for d in y_order + [0]:
        rows = slice(d * y_rows, (d + 1) * y_rows)
        part = pacc[rows, :] + chip_part(near_x[-1], rows)
        if d:
            ysend[d - 1] = part.astype(BF16)
            send_y(0, d)
        else:
            yown[...] = part
    for d in y_order:
        send_y(1, d)

    first_part = chunks * PART // 8
    pair_setup()
    for q in range(first_part):
        pair_first(q)
    if first_part == chunks:
        pair_sends()

    for g, (lo, hi) in enumerate(parts):
        rows = slice(lo * z_rows, hi * z_rows)
        total = yown[rows, :]
        for d in range(1, N_Y):
            waits[("y", (g, d))].wait_recv()
            total = total + yrecv[d - 1, rows].astype(F32)
        for p in range(hi - 1, lo - 1, -1):
            block = total[(p - lo) * z_rows : (p - lo + 1) * z_rows, :]
            d = dz_at[p]
            if d:
                zsend[d - 1] = block.astype(BF16)
                send("z", d, copy(zsend.at[d - 1], zrecv.at[d - 1], z_s.at[d - 1], z_r.at[d - 1], at_z(d)))
            else:
                mine = block
    for q in range(first_part, chunks):
        pair_first(q)
    if first_part < chunks:
        pair_sends()

    for s in range(group):
        gfct[:, s * atoms : (s + 1) * atoms] = jnp.transpose(gfc[s].astype(F32)).astype(BF16)

    for d in range(1, n_z):
        waits[("z", d)].wait_recv()
        mine = mine + zrecv[d - 1].astype(F32)
    mine = nu * mine
    loads["filter"].wait()
    kf = jnp.concatenate([kf8[...], kf8[...]], axis=0)
    wbuf[0, 0] = jnp.concatenate([kf * mine[:, chan : 2 * chan], kf * mine[:, 0:chan]], axis=1).astype(BF16)
    z_order = dz_at[:0:-1]
    for d in z_order:
        there = n_z - d
        to = wbuf.at[0, place_of[there]]
        send("za", there, copy(wbuf.at[0, 0], to, za_s.at[d - 1], za_r.at[there - 1], at_z(d)))
    o_filter[...] = (
        mine[0:EDGE, 0:chan] * mine[0:EDGE, chan : 2 * chan]
        + mine[EDGE : 2 * EDGE, 0:chan] * mine[EDGE : 2 * EDGE, chan : 2 * chan]
    )

    for q in range(chunks):
        pair_second(q)
    dgp[...] = jnp.concatenate([dbp[:, atoms:buf_rows], jnp.zeros((8, 2 * atoms - buf_rows), F32)], axis=1)
    for g in range(4):
        send("rf", g, copy(dbf.at[pl.ds(atoms + g * face, face)], retf.at[g], rf_s.at[g], rf_r.at[g], at_dom[g]))
        send("rp", g, copy(dgp, retp.at[g], rp_s.at[g], rp_r.at[g], at_dom[g]))

    for p in xc:
        waits[("pa", slot_of[p])].wait_recv()
    piece_sum = pw_a[my_piece]
    for s in range(group - 1):
        piece_sum = piece_sum + pw_ar[s]
    pw_b[...] = piece_sum
    for d in z_order:
        send("pb", d, copy(pw_b, pw_br.at[d - 1], pb_s.at[d - 1], pb_r.at[d - 1], at_z(d)))

    for g in (1, 0):
        lo, hi = parts[g]
        for p in range(max(lo, 1), hi):
            waits[("za", dz_at[p])].wait_recv()
        for d in y_order:
            there = N_Y - d
            i = 2 * there - 2 + g
            blocks = pl.ds(lo, hi - lo)
            to = wbuf.at[there, blocks]
            send("ya", (g, there), copy(wbuf.at[0, blocks], to, ya_s.at[2 * d - 2 + g], ya_r.at[i], at_y(d)))

    for d in range(1, n_z):
        waits[("pb", d)].wait_recv()
        piece_sum = piece_sum + pw_br[d - 1]
    pw_c[...] = piece_sum
    for d in y_order:
        send("pc", d, copy(pw_c, pw_cr.at[d - 1], pc_s.at[d - 1], pc_r.at[d - 1], at_y(d)))

    for g in range(4):
        waits[("rf", g)].wait_recv()
        waits[("rp", g)].wait_recv()
    lane = lax.broadcasted_iota(jnp.int32, (8, atoms), 1)
    short_pos = dbp[:, 0:atoms] + ownp[...]
    for g in range(4):
        f = g ^ 1
        moved = pltpu.roll(retp[g], (atoms - face if g % 2 else face), axis=1)
        short_pos = short_pos + jnp.where((lane >= f * face) & (lane < (f + 1) * face), moved, 0.0)
        rows = slice(f * face, (f + 1) * face)
        dbf[rows, :] += retf[g]
    ownp[...] = short_pos

    def turned(d):
        return jnp.transpose(wbuf[d].reshape(y_rows, 2 * chan)[:, 0:chan].astype(F32)).astype(BF16)

    def give_back(d, fg_t, first, count):
        lanes = slice(first * atoms, (first + count) * atoms)
        rows = slice(d * y_rows, (d + 1) * y_rows)
        w = wbuf[d].reshape(y_rows, 2 * chan)
        d_feat_t = nn(fg_t, csh[rows, lanes])
        pq = nn(w, gfct[:, lanes]).reshape(-1, 2, EDGE, count * atoms)
        cs = csf[d * y_rows // EDGE : (d + 1) * y_rows // EDGE, :, lanes].reshape(-1, 2, EDGE, count * atoms)
        wave = (cs[:, 0] * pq[:, 1] - cs[:, 1] * pq[:, 0]).reshape(half, count * atoms)
        hi = wave.astype(BF16).astype(F32)
        d_pos = mu * nn(krow[d], jnp.concatenate([hi, wave - hi], axis=0).astype(BF16))
        return d_feat_t, d_pos

    for d in [0] + y_order[::-1][:-1]:
        if d:
            waits[("ya", (1, d))].wait_recv()
            waits[("ya", (0, d))].wait_recv()
        fg_t = turned(d)
        for first in range(0, group, 2):
            lanes = slice(first * atoms, (first + 2) * atoms)
            d_feat_t, d_pos = give_back(d, fg_t, first, 2)
            if d:
                facc[:, lanes] += d_feat_t
                xacc[:, lanes] += d_pos
            else:
                facc[:, lanes] = d_feat_t
                xacc[:, lanes] = d_pos
    last = y_order[0]
    waits[("ya", (1, last))].wait_recv()
    waits[("ya", (0, last))].wait_recv()
    fg_last = turned(last)

    for d in range(1, N_Y):
        waits[("pc", d)].wait_recv()
        piece_sum = piece_sum + pw_cr[d - 1]
    pw_d[my_piece] = nu * piece_sum
    for p in far_first:
        s = slot_of[p]
        send("pd", s, copy(pw_d.at[my_piece], pw_d.at[my_piece], pd_s.at[s - 1], pd_r.at[s - 1], at_xc(*p)))

    def whole(s):
        lanes = slice(s * atoms, (s + 1) * atoms)
        d_feat_t, d_pos = give_back(last, fg_last, s, 1)
        return facc[:, lanes] + d_feat_t, xacc[:, lanes] + d_pos

    for dx in x_order + [0]:
        d_feat_t, d_pos = whole(dx * N_CORE + 1)
        outs_c[dx, 0:chan] = d_feat_t
        outs_c[dx, chan:] = d_pos
        send("oc", dx, copy(outs_c.at[dx], outr_c.at[dx], oc_s.at[dx], oc_r.at[dx], at_xc(0, 1)))
    for dx in x_order:
        d_feat_t, d_pos = whole(dx * N_CORE)
        waits[("oc", dx)].wait_recv()
        d_feat_t = d_feat_t + outr_c[dx, 0:chan]
        d_pos = d_pos + outr_c[dx, chan:]
        pos_hi = d_pos.astype(BF16).astype(F32)
        outs_x[dx - 1] = jnp.concatenate([d_feat_t, pos_hi, d_pos - pos_hi], axis=0).astype(BF16)
        send("ox", dx, copy(outs_x.at[dx - 1], outr_x.at[dx - 1], ox_s.at[dx - 1], ox_r.at[dx - 1], at_xc(N_X - dx, 0)))

    long_t, long_pos = whole(0)
    waits[("oc", 0)].wait_recv()
    long_t = long_t + outr_c[0, 0:chan]
    long_pos = long_pos + outr_c[0, chan:]
    late = [waits[("ox", dx)] for dx in x_order]
    for c in sent:
        if all(c is not other for other in late):
            c.wait_send()
    for p in xc:
        waits[("pd", slot_of[p])].wait_recv()
    for j in range(group):
        o_out[j * out_rows : (j + 1) * out_rows, :] = pw_d[j, 0:out_rows]
        o_radial[j * rad_rows : (j + 1) * rad_rows, :] = pw_d[j, out_rows : out_rows + rad_rows]
    for dx in near_x:
        waits[("ox", dx)].wait_recv()
        got = outr_x[dx - 1].astype(F32)
        long_t = long_t + got[0:chan]
        long_pos = long_pos + got[chan : chan + 8] + got[chan + 8 : chan + 16]
    o_feat[...] = jnp.transpose(long_t) + dbf[0:atoms, :]
    o_pos[...] = (long_pos + ownp[...])[0:3]
    for c in late:
        c.wait_send()


def store(*refs):
    n = len(refs) // 2
    for src, dst in zip(refs[:n], refs[n:]):
        dst[...] = src[...]


def shards(features, cotangent, positions, neighbours, counts, k_index, k_filter, w_radial, w_out):
    n_slab = lax.axis_size("slab")
    atoms, chan = features.shape
    levels, hidden = w_radial.shape
    group = N_X * N_CORE
    n_z = Z_HI * n_slab
    k_loc = N_Y * n_z * EDGE
    face = atoms // 8
    buf_rows = atoms + 4 * face
    piece = hidden // group + 8
    pairs = atoms * neighbours.shape[0]
    v = pltpu.VMEM
    dma = pltpu.SemaphoreType.DMA
    scratch = [
        v(positions.shape, F32),
        v(neighbours.shape, jnp.int32),
        v((1, atoms), jnp.int32),
        v(k_index.shape, jnp.int32),
        v(w_radial.shape, BF16),
        v(w_out.shape, BF16),
        v((group, atoms, 2 * chan), BF16),
        v((group, 8, atoms), F32),
        v((4, face, chan), BF16),
        v((4, 8, atoms), F32),
        v((2 * k_loc // EDGE, EDGE, group * atoms), F32),
        v((2 * k_loc, group * atoms), BF16),
        v((N_Y - 1, 2 * n_z * EDGE, 2 * chan), BF16),
        v((2 * n_z * EDGE, 2 * chan), F32),
        v((N_Y - 1, 2 * n_z * EDGE, 2 * chan), BF16),
        v((n_z - 1, 2 * EDGE, 2 * chan), BF16),
        v((n_z - 1, 2 * EDGE, 2 * chan), BF16),
        v((N_Y, n_z, 2 * EDGE, 2 * chan), BF16),
        v((EDGE, chan), F32),
        v((k_loc, k_index.shape[1]), BF16),
        v((2 * chan, group * atoms), BF16),
        v((buf_rows, pairs), BF16),
        v((hidden, pairs), BF16),
        v((hidden, pairs), BF16),
        v((levels, pairs), F32),
        v((8, pairs), F32),
        v((8, pairs), F32),
        v((2 * k_loc, 2 * chan), F32),
        v((chan, group * atoms), F32),
        v((8, group * atoms), F32),
        v((N_X, chan + 8, atoms), F32),
        v((N_X, chan + 8, atoms), F32),
        v((N_X - 1, chan + 16, atoms), BF16),
        v((N_X - 1, chan + 16, atoms), BF16),
        v((k_loc, 32), BF16),
        v((N_Y, 8, 2 * n_z * EDGE), BF16),
        v((chan, 2 * atoms), BF16),
        v((32, 2 * atoms), BF16),
        v((chan, atoms), F32),
        v((hidden, 128), BF16),
        v((chan, hidden), BF16),
        v((buf_rows, chan), F32),
        v((8, buf_rows), F32),
        v((8, atoms), F32),
        v((8, atoms), F32),
        v((hidden, chan), F32),
        v((levels, hidden), F32),
        v((4, face, chan), F32),
        v((4, 8, atoms), F32),
        v((group, piece, chan), F32),
        v((group - 1, piece, chan), F32),
        v((piece, chan), F32),
        v((n_z - 1, piece, chan), F32),
        v((piece, chan), F32),
        v((N_Y - 1, piece, chan), F32),
        v((group, piece, chan), F32),
        dma((9,)),
    ]
    for n in (group - 1, group - 1, 4, 4, 2 * N_Y - 2, n_z - 1, n_z - 1, 2 * N_Y - 2):
        scratch += [dma((n,)), dma((n,))]
    for n in (N_X, N_X - 1, 4, 4, group - 1, n_z - 1, N_Y - 1, group - 1):
        scratch += [dma((n,)), dma((n,))]
    hbm = pl.BlockSpec(memory_space=pltpu.HBM)
    vmem = pl.BlockSpec(memory_space=pltpu.VMEM)
    shapes = (
        jax.ShapeDtypeStruct((atoms, chan), F32),
        jax.ShapeDtypeStruct((3, atoms), F32),
        jax.ShapeDtypeStruct((EDGE, chan), F32),
        jax.ShapeDtypeStruct((levels, hidden), F32),
        jax.ShapeDtypeStruct((hidden, chan), F32),
    )
    results = pl.pallas_call(
        functools.partial(body, n_slab),
        out_shape=shapes,
        in_specs=[hbm] * 9,
        out_specs=(vmem,) * 5,
        scratch_shapes=scratch,
        compiler_params=pltpu.CompilerParams(
            collective_id=0, has_side_effects=True, vmem_limit_bytes=40 << 20
        ),
        name="ewald",
    )(
        *(
            pltpu.with_memory_space_constraint(v, pltpu.HBM)
            for v in (
                features,
                cotangent,
                positions,
                neighbours,
                counts.reshape(1, atoms),
                k_index,
                k_filter,
                w_radial,
                w_out,
            )
        )
    )
    return pl.pallas_call(
        store,
        out_shape=shapes,
        in_specs=[vmem] * 5,
        out_specs=(vmem,) * 5,
        compiler_params=pltpu.CompilerParams(vmem_limit_bytes=40 << 20),
        name="store",
    )(*results)


def solution(mesh):
    both = ("dom", "slab")
    in_specs = (P(both, None), P(both, None), P(None, both), P(None, both), P(both), P(), P(), P(), P())
    out_specs = (P(both, None), P(None, both), P(both, None), P(), P())
    return jax.shard_map(shards, mesh=mesh, in_specs=in_specs, out_specs=out_specs, check_vma=False)
```

```python
import functools
import math

import jax
import jax.numpy as jnp
from jax import lax
from jax.experimental import pallas as pl
from jax.experimental.pallas import tpu as pltpu
from jax.sharding import PartitionSpec as P

Z_HI, N_X, N_Y, N_CORE = 2, 4, 4, 2
EDGE = 8
PART = 8
BEFORE = 2
NEAR = 5
F32 = jnp.float32
BF16 = jnp.bfloat16

SIN_C = (3.1415926401307077, -5.167710083507896, 2.550077523214726, -0.5982912856213906, 0.07765766030763246)
COS_C = (
    0.9999999997799044,
    -4.934802137078806,
    4.058709159555702,
    -1.3352120030438075,
    0.23493731378604543,
    -0.024396324301093893,
)


def horner(coefs, u):
    y = coefs[-1] * u + coefs[-2]
    for k in coefs[-3::-1]:
        y = y * u + k
    return y


def turns(t):
    r = t - jnp.round(t)
    u = r * r
    s = r * horner(SIN_C, u)
    c = horner(COS_C, u)
    return 1.0 - 2.0 * (s * s), 2.0 * (s * c)


def split3(v):
    hi = v.astype(BF16)
    rest = v - hi.astype(F32)
    mid = rest.astype(BF16)
    lo = (rest - mid.astype(F32)).astype(BF16)
    return jnp.concatenate([hi.astype(F32), mid.astype(F32), lo.astype(F32), jnp.zeros_like(v)], axis=0).astype(BF16)


def nn(a, b):
    return lax.dot_general(a, b, (((1,), (0,)), ((), ())), preferred_element_type=F32)


def nt(a, b):
    return lax.dot_general(a, b, (((1,), (1,)), ((), ())), preferred_element_type=F32)


def body(
    n_slab,
    feat_hbm,
    cot_hbm,
    pos_hbm,
    nbr_hbm,
    cnt_hbm,
    kidx_hbm,
    kfil_hbm,
    wrad_hbm,
    wout_hbm,
    o_feat,
    o_pos,
    o_filter,
    o_radial,
    o_out,
    pos_ref,
    nbr_ref,
    cnt_ref,
    kidx_ref,
    wrad_ref,
    wout_ref,
    gfc,
    gpos,
    hfeat,
    hpos,
    csf,
    csh,
    ysend,
    yown,
    yrecv,
    zsend,
    zrecv,
    wbuf,
    kf8,
    picked,
    gfct,
    hot_s,
    act_s,
    dpre_s,
    rbf_s,
    chord_s,
    cosine_s,
    pacc,
    facc,
    xacc,
    outs_c,
    outr_c,
    outs_x,
    outr_x,
    kcol,
    krow,
    bufft,
    possp,
    cott,
    wradt,
    woutt,
    dbf,
    dbp,
    dgp,
    ownp,
    pwo,
    pwr,
    retf,
    retp,
    pw_a,
    pw_ar,
    pw_b,
    pw_br,
    pw_c,
    pw_cr,
    pw_d,
    loc_sem,
    g_s,
    g_r,
    gp_s,
    gp_r,
    h_s,
    h_r,
    hp_s,
    hp_r,
    y_s,
    y_r,
    z_s,
    z_r,
    za_s,
    za_r,
    ya_s,
    ya_r,
    oc_s,
    oc_r,
    ox_s,
    ox_r,
    rf_s,
    rf_r,
    rp_s,
    rp_r,
    pa_s,
    pa_r,
    pb_s,
    pb_r,
    pc_s,
    pc_r,
    pd_s,
    pd_r,
):
    atoms, chan = feat_hbm.shape
    slots = nbr_ref.shape[0]
    k_total = kidx_ref.shape[1]
    n_z = Z_HI * n_slab
    group = N_X * N_CORE
    k_loc = N_Y * n_z * EDGE
    n_dom = Z_HI * N_X * N_Y * N_CORE
    face = atoms // 8
    buf_rows = atoms + 4 * face
    nu = 1.0 / math.sqrt(atoms * n_dom * n_slab)
    mu = 1.0 / math.sqrt(k_total)

    dom = lax.axis_index("dom")
    slab = lax.axis_index("slab")
    core = lax.rem(dom, N_CORE)
    y = lax.rem(lax.div(dom, N_CORE), N_Y)
    x = lax.rem(lax.div(dom, N_CORE * N_Y), N_X)
    zh = lax.div(dom, N_CORE * N_Y * N_X)
    z = zh * n_slab + slab

    def dom_of(zh_, x_, y_, c_):
        return ((zh_ * N_X + x_) * N_Y + y_) * N_CORE + c_

    def at_xc(dx, dc):
        return (dom_of(zh, lax.rem(x + dx, N_X), y, lax.rem(core + dc, N_CORE)), slab)

    def at_y(d):
        return (dom_of(zh, x, lax.rem(y + d, N_Y), core), slab)

    def at_z(d):
        zz = lax.rem(z + d, n_z)
        return (dom_of(lax.div(zz, n_slab), x, y, core), lax.rem(zz, n_slab))

    at_dom = (
        (lax.rem(dom + n_dom - 1, n_dom), slab),
        (lax.rem(dom + 1, n_dom), slab),
        (dom, lax.rem(slab + n_slab - 1, n_slab)),
        (dom, lax.rem(slab + 1, n_slab)),
    )

    def copy(src, dst, ss, rs, dev):
        return pltpu.make_async_remote_copy(
            src_ref=src, dst_ref=dst, send_sem=ss, recv_sem=rs, device_id=dev, device_id_type=pl.DeviceIdType.MESH
        )

    xc = [(dx, dc) for dx in range(N_X) for dc in range(N_CORE)][1:]
    slot_of = {p: p[0] * N_CORE + p[1] for p in xc}
    far_first = sorted(xc, key=lambda p: -min(p[0], N_X - p[0]))
    near_first = far_first[::-1]

    peers = [at_xc(*p) for p in xc] + [at_y(d) for d in range(1, N_Y)] + [at_z(d) for d in range(1, n_z)]
    peers += [at_dom[0], at_dom[1]]
    barrier = pltpu.get_barrier_semaphore()
    for dev in peers:
        pl.semaphore_signal(barrier, inc=1, device_id=dev, device_id_type=pl.DeviceIdType.MESH)

    k_first = pl.multiple_of((dom * n_slab + slab) * EDGE, EDGE)
    loads = {}
    for i, (name, src, dst) in enumerate(
        (
            ("pos", pos_hbm, pos_ref),
            ("feat", feat_hbm, gfc.at[0, :, pl.ds(0, chan)]),
            ("cot", cot_hbm, gfc.at[0, :, pl.ds(chan, chan)]),
            ("kidx", kidx_hbm, kidx_ref),
            ("nbr", nbr_hbm, nbr_ref),
            ("cnt", cnt_hbm, cnt_ref),
            ("wrad", wrad_hbm, wrad_ref),
            ("wout", wout_hbm, wout_ref),
            ("filter", kfil_hbm.at[pl.ds(k_first, EDGE)], kf8),
        )
    ):
        loads[name] = pltpu.make_async_copy(src, dst, loc_sem.at[i])
        loads[name].start()
    m = lax.broadcasted_iota(jnp.int32, (k_loc, 1), 0)
    e = jnp.bitwise_and(m, EDGE - 1)
    place = lax.rem(lax.div(m, EDGE), n_z)
    bz = lax.rem(jnp.where(lax.rem(place, 2) == 1, lax.div(place + 1, 2), n_z - lax.div(place, 2)) + z, n_z)
    by = lax.rem(lax.div(m, EDGE * n_z) + y, N_Y)
    row = (dom_of(lax.div(bz, n_slab), x, by, core) * n_slab + lax.rem(bz, n_slab)) * EDGE + e
    column = lax.broadcasted_iota(jnp.int32, (k_loc, k_total), 1)
    picked[...] = jnp.where(row == column, 1.0, 0.0).astype(BF16)
    gpos[0] = jnp.zeros((8, atoms), F32)
    loads["pos"].wait()
    gpos[0, 0:3] = pos_ref[...]

    pl.semaphore_wait(barrier, len(peers))

    sent = []
    waits = {}

    def send(name, key, c):
        c.start()
        sent.append(c)
        waits[(name, key)] = c

    for p in far_first:
        s = slot_of[p]
        send("gp", s, copy(gpos.at[0], gpos.at[s], gp_s.at[s - 1], gp_r.at[s - 1], at_xc(*p)))
    loads["feat"].wait()
    loads["cot"].wait()
    x_order = sorted(range(1, N_X), key=lambda d: -min(d, N_X - d))
    for dx in x_order:
        s = dx * N_CORE
        send("g", s, copy(gfc.at[0], gfc.at[s], g_s.at[s - 1], g_r.at[s - 1], at_xc(dx, 0)))
    send("g", 1, copy(gfc.at[0], gfc.at[1], g_s.at[0], g_r.at[0], at_xc(0, 1)))
    for g in range(4):
        f = g ^ 1
        dev = at_dom[f]
        mine = gfc.at[0, pl.ds(f * face, face), pl.ds(0, chan)]
        send("h", g, copy(mine, hfeat.at[g], h_s.at[g], h_r.at[g], dev))
        send("hp", g, copy(gpos.at[0], hpos.at[g], hp_s.at[g], hp_r.at[g], dev))
    loads["kidx"].wait()

    pick = picked[...]
    k8 = jnp.concatenate([kidx_ref[...].astype(F32), jnp.zeros((5, k_total), F32)], axis=0)
    half = n_z * EDGE
    for d in range(N_Y):
        block = pick[d * half : (d + 1) * half]
        krow[d] = nt(k8.astype(BF16), jnp.concatenate([block, block], axis=0)).astype(BF16)
    kcol[...] = nt(pick, jnp.concatenate([k8, k8, k8, jnp.zeros_like(k8)], axis=0).astype(BF16)).astype(BF16)

    def tables(s):
        t = nn(kcol[...], split3(gpos[s]))
        cosine, sine = turns(t)
        lanes = slice(s * atoms, (s + 1) * atoms)
        both = jnp.stack([cosine.reshape(-1, EDGE, atoms), sine.reshape(-1, EDGE, atoms)], axis=1)
        csf[:, :, lanes] = both.reshape(-1, EDGE, atoms)
        csh[:, lanes] = both.reshape(-1, atoms).astype(BF16)

    tables(0)
    for p in near_first:
        s = slot_of[p]
        waits[("gp", s)].wait_recv()
        tables(s)

    def pair_setup():
        for g in range(4):
            waits[("h", g)].wait_recv()
            waits[("hp", g)].wait_recv()
        for name in ("nbr", "cnt", "wrad", "wout"):
            loads[name].wait()
        own_t = jnp.transpose(gfc[0, :, 0:chan].astype(F32))
        ghost = jnp.concatenate([hfeat[...].reshape(4 * face, chan), jnp.zeros((atoms - 4 * face, chan), BF16)], axis=0)
        ghost_t = jnp.transpose(ghost.astype(F32))
        bufft[...] = jnp.concatenate([own_t, ghost_t], axis=1).astype(BF16)
        cott[...] = jnp.transpose(gfc[0, :, chan : 2 * chan].astype(F32))
        wradt[...] = jnp.transpose(
            jnp.concatenate([wrad_ref[...].astype(F32), jnp.zeros((128 - wrad_ref.shape[0], 128), F32)], axis=0)
        ).astype(BF16)
        woutt[...] = jnp.transpose(wout_ref[...].astype(F32)).astype(BF16)
        lane = lax.broadcasted_iota(jnp.int32, (8, atoms), 1)
        ghost_pos = jnp.zeros((8, atoms), F32)
        for g in range(4):
            moved = pltpu.roll(hpos[g], (face if g % 2 else atoms - face), axis=1)
            ghost_pos = jnp.where((lane >= g * face) & (lane < (g + 1) * face), moved, ghost_pos)
        possp[:, 0:atoms] = split3(gpos[0])
        possp[:, atoms : 2 * atoms] = split3(ghost_pos)
        for ref in (dbf, dbp, ownp, pwo, pwr):
            ref[...] = jnp.zeros(ref.shape, F32)

    levels = wrad_ref.shape[0]
    rates = 0.5 * jnp.exp(
        lax.broadcasted_iota(jnp.int32, (levels, 1), 0).astype(F32) * (math.log(16.0) / (levels - 1))
    )

    span = 2
    width = span * atoms

    def weights(first):
        return jnp.concatenate(
            [cott[...] * jnp.where(cnt_ref[...] > first + j, slots**-0.5, 0.0) for j in range(span)], axis=1
        )

    def pair_first(q):
        first = q * span
        here = slice(q * width, (q + 1) * width)
        idx = jnp.concatenate([nbr_ref[first + j : first + j + 1, :] for j in range(span)], axis=1)
        hot = jnp.where(lax.broadcasted_iota(jnp.int32, (buf_rows, width), 0) == idx, 1.0, 0.0).astype(BF16)
        tp = nn(possp[:, 0:buf_rows], hot)
        target = tp[0:8] + tp[8:16] + tp[16:24]
        source = jnp.concatenate([gpos[0]] * span, axis=1)
        cosine, chord = turns(target - source)
        dist2 = jnp.sum(chord * chord, axis=0, keepdims=True)
        rbf = jnp.exp(-rates * dist2)
        rbf_h = rbf.astype(BF16)
        pre = nn(wradt[:, 0:levels], rbf_h)
        gate = 0.5 * jnp.tanh(0.5 * pre) + 0.5
        act = (pre * gate).astype(BF16)
        dphi = (weights(first) * nn(bufft[:, 0:buf_rows], hot)).astype(BF16)
        pwo[...] += nt(act, dphi)
        d_act = nn(wout_ref[...], dphi)
        dpre = (d_act * gate * (1.0 + pre * (1.0 - gate))).astype(BF16)
        pwr[...] += nt(rbf_h, dpre)
        hot_s[:, here] = hot
        act_s[:, here] = act
        dpre_s[:, here] = dpre
        rbf_s[:, here] = rbf
        chord_s[:, here] = chord
        cosine_s[:, here] = cosine

    def pair_second(q):
        here = slice(q * width, (q + 1) * width)
        hot = hot_s[:, here]
        given = weights(q * span) * nn(woutt[...], act_s[:, here])
        given_hi = given.astype(BF16)
        given_lo = (given - given_hi.astype(F32)).astype(BF16)
        added = nt(hot, jnp.concatenate([given_hi, given_lo], axis=0))
        dbf[...] += added[:, 0:chan] + added[:, chan : 2 * chan]
        d_rbf = nn(wrad_ref[...], dpre_s[:, here])
        d_chord2 = -jnp.sum(d_rbf * rates * rbf_s[:, here], axis=0, keepdims=True)
        dmove = (2.0 * mu) * d_chord2 * chord_s[:, here] * cosine_s[:, here]
        move_hi = dmove.astype(BF16).astype(F32)
        moves = nt(jnp.concatenate([move_hi, dmove - move_hi], axis=0).astype(BF16), hot)
        dbp[...] += moves[0:8] + moves[8:16]
        for j in range(span):
            ownp[...] -= dmove[:, j * atoms : (j + 1) * atoms]

    out_rows = pwo.shape[0] // group
    rad_rows = levels // group
    my_piece = x * N_CORE + core

    def pair_sends():
        for j in range(group):
            pw_a[j, 0:out_rows] = pwo[j * out_rows : (j + 1) * out_rows, :]
            tail = pwr[j * rad_rows : (j + 1) * rad_rows, :]
            pw_a[j, out_rows:] = jnp.concatenate([tail, jnp.zeros((8 - rad_rows, tail.shape[1]), F32)], axis=0)
        for p in far_first:
            s = slot_of[p]
            piece = lax.rem(x + p[0], N_X) * N_CORE + lax.rem(core + p[1], N_CORE)
            send("pa", s, copy(pw_a.at[piece], pw_ar.at[s - 1], pa_s.at[s - 1], pa_r.at[s - 1], at_xc(*p)))

    def hand_over(dx):
        s = dx * N_CORE
        waits[("g", s)].wait_recv()
        send("g", s + 1, copy(gfc.at[s], gfc.at[s + 1], g_s.at[s], g_r.at[s], at_xc(0, 1)))

    def chip_part(dx, rows):
        lanes = slice(dx * N_CORE * atoms, (dx + 1) * N_CORE * atoms)
        return nn(csh[rows, lanes], gfc[dx * N_CORE : (dx + 1) * N_CORE].reshape(N_CORE * atoms, 2 * chan))

    dz_at = [(p + 1) // 2 if p % 2 else (n_z - p // 2) % n_z for p in range(n_z)]
    place_of = {dz: p for p, dz in enumerate(dz_at)}
    z_rows = 2 * EDGE
    near_z = n_z * NEAR // 8
    parts = ((near_z, n_z), (0, near_z))
    y_rows = n_z * 2 * EDGE
    near_x = x_order[::-1]
    all_rows = slice(0, 2 * k_loc)
    chunks = slots // 2
    for dx in near_x[:-1]:
        hand_over(dx)
    waits[("g", 1)].wait_recv()
    pacc[...] = chip_part(0, all_rows)
    hand_over(near_x[-1])
    for dx in near_x[:-1]:
        waits[("g", dx * N_CORE + 1)].wait_recv()
        pacc[...] += chip_part(dx, all_rows)
    waits[("g", near_x[-1] * N_CORE + 1)].wait_recv()
    y_order = sorted(range(1, N_Y), key=lambda d: -min(d, N_Y - d))

    def send_y(g, d):
        rows = pl.ds(parts[g][0] * z_rows, (parts[g][1] - parts[g][0]) * z_rows)
        i = 2 * d - 2 + g
        send("y", (g, d), copy(ysend.at[d - 1, rows], yrecv.at[d - 1, rows], y_s.at[i], y_r.at[i], at_y(d)))

    for d in y_order + [0]:
        rows = slice(d * y_rows, (d + 1) * y_rows)
        part = pacc[rows, :] + chip_part(near_x[-1], rows)
        if d:
            ysend[d - 1] = part.astype(BF16)
            send_y(0, d)
        else:
            yown[...] = part
    for d in y_order:
        send_y(1, d)

    first_part = chunks * PART // 8
    pair_setup()
    for q in range(first_part):
        pair_first(q)
    if first_part == chunks:
        pair_sends()

    for g, (lo, hi) in enumerate(parts):
        rows = slice(lo * z_rows, hi * z_rows)
        total = yown[rows, :]
        for d in range(1, N_Y):
            waits[("y", (g, d))].wait_recv()
            total = total + yrecv[d - 1, rows].astype(F32)
        for p in range(hi - 1, lo - 1, -1):
            block = total[(p - lo) * z_rows : (p - lo + 1) * z_rows, :]
            d = dz_at[p]
            if d:
                zsend[d - 1] = block.astype(BF16)
                send("z", d, copy(zsend.at[d - 1], zrecv.at[d - 1], z_s.at[d - 1], z_r.at[d - 1], at_z(d)))
            else:
                mine = block
    for q in range(first_part, chunks):
        pair_first(q)
    if first_part < chunks:
        pair_sends()

    for s in range(group):
        gfct[:, s * atoms : (s + 1) * atoms] = jnp.transpose(gfc[s].astype(F32)).astype(BF16)

    for d in range(1, n_z):
        waits[("z", d)].wait_recv()
        mine = mine + zrecv[d - 1].astype(F32)
    mine = nu * mine
    loads["filter"].wait()
    kf = jnp.concatenate([kf8[...], kf8[...]], axis=0)
    wbuf[0, 0] = jnp.concatenate([kf * mine[:, chan : 2 * chan], kf * mine[:, 0:chan]], axis=1).astype(BF16)
    z_order = dz_at[:0:-1]
    for d in z_order:
        there = n_z - d
        to = wbuf.at[0, place_of[there]]
        send("za", there, copy(wbuf.at[0, 0], to, za_s.at[d - 1], za_r.at[there - 1], at_z(d)))
    o_filter[...] = (
        mine[0:EDGE, 0:chan] * mine[0:EDGE, chan : 2 * chan]
        + mine[EDGE : 2 * EDGE, 0:chan] * mine[EDGE : 2 * EDGE, chan : 2 * chan]
    )

    before = chunks * BEFORE // 8
    for q in range(before):
        pair_second(q)
    for p in xc:
        waits[("pa", slot_of[p])].wait_recv()
    piece_sum = pw_a[my_piece]
    for s in range(group - 1):
        piece_sum = piece_sum + pw_ar[s]
    pw_b[...] = piece_sum
    for d in z_order:
        send("pb", d, copy(pw_b, pw_br.at[d - 1], pb_s.at[d - 1], pb_r.at[d - 1], at_z(d)))
    for q in range(before, chunks):
        pair_second(q)
    dgp[...] = jnp.concatenate([dbp[:, atoms:buf_rows], jnp.zeros((8, 2 * atoms - buf_rows), F32)], axis=1)
    for g in range(4):
        send("rf", g, copy(dbf.at[pl.ds(atoms + g * face, face)], retf.at[g], rf_s.at[g], rf_r.at[g], at_dom[g]))
        send("rp", g, copy(dgp, retp.at[g], rp_s.at[g], rp_r.at[g], at_dom[g]))

    for g in (1, 0):
        lo, hi = parts[g]
        for p in range(max(lo, 1), hi):
            waits[("za", dz_at[p])].wait_recv()
        for d in y_order:
            there = N_Y - d
            i = 2 * there - 2 + g
            blocks = pl.ds(lo, hi - lo)
            to = wbuf.at[there, blocks]
            send("ya", (g, there), copy(wbuf.at[0, blocks], to, ya_s.at[2 * d - 2 + g], ya_r.at[i], at_y(d)))

    for d in range(1, n_z):
        waits[("pb", d)].wait_recv()
        piece_sum = piece_sum + pw_br[d - 1]
    pw_c[...] = piece_sum
    for d in y_order:
        send("pc", d, copy(pw_c, pw_cr.at[d - 1], pc_s.at[d - 1], pc_r.at[d - 1], at_y(d)))

    for g in range(4):
        waits[("rf", g)].wait_recv()
        waits[("rp", g)].wait_recv()
    lane = lax.broadcasted_iota(jnp.int32, (8, atoms), 1)
    short_pos = dbp[:, 0:atoms] + ownp[...]
    for g in range(4):
        f = g ^ 1
        moved = pltpu.roll(retp[g], (atoms - face if g % 2 else face), axis=1)
        short_pos = short_pos + jnp.where((lane >= f * face) & (lane < (f + 1) * face), moved, 0.0)
        rows = slice(f * face, (f + 1) * face)
        dbf[rows, :] += retf[g]
    ownp[...] = short_pos

    def turned(d):
        return jnp.transpose(wbuf[d].reshape(y_rows, 2 * chan)[:, 0:chan].astype(F32)).astype(BF16)

    def give_back(d, fg_t, first, count):
        lanes = slice(first * atoms, (first + count) * atoms)
        rows = slice(d * y_rows, (d + 1) * y_rows)
        w = wbuf[d].reshape(y_rows, 2 * chan)
        d_feat_t = nn(fg_t, csh[rows, lanes])
        pq = nn(w, gfct[:, lanes]).reshape(-1, 2, EDGE, count * atoms)
        cs = csf[d * y_rows // EDGE : (d + 1) * y_rows // EDGE, :, lanes].reshape(-1, 2, EDGE, count * atoms)
        wave = (cs[:, 0] * pq[:, 1] - cs[:, 1] * pq[:, 0]).reshape(half, count * atoms)
        hi = wave.astype(BF16).astype(F32)
        d_pos = mu * nn(krow[d], jnp.concatenate([hi, wave - hi], axis=0).astype(BF16))
        return d_feat_t, d_pos

    for d in [0] + y_order[::-1][:-1]:
        if d:
            waits[("ya", (1, d))].wait_recv()
            waits[("ya", (0, d))].wait_recv()
        fg_t = turned(d)
        for first in range(0, group, 2):
            lanes = slice(first * atoms, (first + 2) * atoms)
            d_feat_t, d_pos = give_back(d, fg_t, first, 2)
            if d:
                facc[:, lanes] += d_feat_t
                xacc[:, lanes] += d_pos
            else:
                facc[:, lanes] = d_feat_t
                xacc[:, lanes] = d_pos
    for d in range(1, N_Y):
        waits[("pc", d)].wait_recv()
        piece_sum = piece_sum + pw_cr[d - 1]
    pw_d[my_piece] = nu * piece_sum
    for p in far_first:
        s = slot_of[p]
        send("pd", s, copy(pw_d.at[my_piece], pw_d.at[my_piece], pd_s.at[s - 1], pd_r.at[s - 1], at_xc(*p)))
    last = y_order[0]
    waits[("ya", (1, last))].wait_recv()
    waits[("ya", (0, last))].wait_recv()
    fg_last = turned(last)

    def whole(s):
        lanes = slice(s * atoms, (s + 1) * atoms)
        d_feat_t, d_pos = give_back(last, fg_last, s, 1)
        return facc[:, lanes] + d_feat_t, xacc[:, lanes] + d_pos

    for dx in x_order + [0]:
        d_feat_t, d_pos = whole(dx * N_CORE + 1)
        outs_c[dx, 0:chan] = d_feat_t
        outs_c[dx, chan:] = d_pos
        send("oc", dx, copy(outs_c.at[dx], outr_c.at[dx], oc_s.at[dx], oc_r.at[dx], at_xc(0, 1)))
    for dx in x_order:
        d_feat_t, d_pos = whole(dx * N_CORE)
        waits[("oc", dx)].wait_recv()
        d_feat_t = d_feat_t + outr_c[dx, 0:chan]
        d_pos = d_pos + outr_c[dx, chan:]
        pos_hi = d_pos.astype(BF16).astype(F32)
        outs_x[dx - 1] = jnp.concatenate([d_feat_t, pos_hi, d_pos - pos_hi], axis=0).astype(BF16)
        send("ox", dx, copy(outs_x.at[dx - 1], outr_x.at[dx - 1], ox_s.at[dx - 1], ox_r.at[dx - 1], at_xc(N_X - dx, 0)))

    long_t, long_pos = whole(0)
    waits[("oc", 0)].wait_recv()
    long_t = long_t + outr_c[0, 0:chan]
    long_pos = long_pos + outr_c[0, chan:]
    late = [waits[("ox", dx)] for dx in x_order]
    for c in sent:
        if all(c is not other for other in late):
            c.wait_send()
    for p in xc:
        waits[("pd", slot_of[p])].wait_recv()
    for j in range(group):
        o_out[j * out_rows : (j + 1) * out_rows, :] = pw_d[j, 0:out_rows]
        o_radial[j * rad_rows : (j + 1) * rad_rows, :] = pw_d[j, out_rows : out_rows + rad_rows]
    for dx in near_x:
        waits[("ox", dx)].wait_recv()
        got = outr_x[dx - 1].astype(F32)
        long_t = long_t + got[0:chan]
        long_pos = long_pos + got[chan : chan + 8] + got[chan + 8 : chan + 16]
    o_feat[...] = jnp.transpose(long_t) + dbf[0:atoms, :]
    o_pos[...] = (long_pos + ownp[...])[0:3]
    for c in late:
        c.wait_send()


def store(*refs):
    n = len(refs) // 2
    for src, dst in zip(refs[:n], refs[n:]):
        dst[...] = src[...]


def shards(features, cotangent, positions, neighbours, counts, k_index, k_filter, w_radial, w_out):
    n_slab = lax.axis_size("slab")
    atoms, chan = features.shape
    levels, hidden = w_radial.shape
    group = N_X * N_CORE
    n_z = Z_HI * n_slab
    k_loc = N_Y * n_z * EDGE
    face = atoms // 8
    buf_rows = atoms + 4 * face
    piece = hidden // group + 8
    pairs = atoms * neighbours.shape[0]
    v = pltpu.VMEM
    dma = pltpu.SemaphoreType.DMA
    scratch = [
        v(positions.shape, F32),
        v(neighbours.shape, jnp.int32),
        v((1, atoms), jnp.int32),
        v(k_index.shape, jnp.int32),
        v(w_radial.shape, BF16),
        v(w_out.shape, BF16),
        v((group, atoms, 2 * chan), BF16),
        v((group, 8, atoms), F32),
        v((4, face, chan), BF16),
        v((4, 8, atoms), F32),
        v((2 * k_loc // EDGE, EDGE, group * atoms), F32),
        v((2 * k_loc, group * atoms), BF16),
        v((N_Y - 1, 2 * n_z * EDGE, 2 * chan), BF16),
        v((2 * n_z * EDGE, 2 * chan), F32),
        v((N_Y - 1, 2 * n_z * EDGE, 2 * chan), BF16),
        v((n_z - 1, 2 * EDGE, 2 * chan), BF16),
        v((n_z - 1, 2 * EDGE, 2 * chan), BF16),
        v((N_Y, n_z, 2 * EDGE, 2 * chan), BF16),
        v((EDGE, chan), F32),
        v((k_loc, k_index.shape[1]), BF16),
        v((2 * chan, group * atoms), BF16),
        v((buf_rows, pairs), BF16),
        v((hidden, pairs), BF16),
        v((hidden, pairs), BF16),
        v((levels, pairs), F32),
        v((8, pairs), F32),
        v((8, pairs), F32),
        v((2 * k_loc, 2 * chan), F32),
        v((chan, group * atoms), F32),
        v((8, group * atoms), F32),
        v((N_X, chan + 8, atoms), F32),
        v((N_X, chan + 8, atoms), F32),
        v((N_X - 1, chan + 16, atoms), BF16),
        v((N_X - 1, chan + 16, atoms), BF16),
        v((k_loc, 32), BF16),
        v((N_Y, 8, 2 * n_z * EDGE), BF16),
        v((chan, 2 * atoms), BF16),
        v((32, 2 * atoms), BF16),
        v((chan, atoms), F32),
        v((hidden, 128), BF16),
        v((chan, hidden), BF16),
        v((buf_rows, chan), F32),
        v((8, buf_rows), F32),
        v((8, atoms), F32),
        v((8, atoms), F32),
        v((hidden, chan), F32),
        v((levels, hidden), F32),
        v((4, face, chan), F32),
        v((4, 8, atoms), F32),
        v((group, piece, chan), F32),
        v((group - 1, piece, chan), F32),
        v((piece, chan), F32),
        v((n_z - 1, piece, chan), F32),
        v((piece, chan), F32),
        v((N_Y - 1, piece, chan), F32),
        v((group, piece, chan), F32),
        dma((9,)),
    ]
    for n in (group - 1, group - 1, 4, 4, 2 * N_Y - 2, n_z - 1, n_z - 1, 2 * N_Y - 2):
        scratch += [dma((n,)), dma((n,))]
    for n in (N_X, N_X - 1, 4, 4, group - 1, n_z - 1, N_Y - 1, group - 1):
        scratch += [dma((n,)), dma((n,))]
    hbm = pl.BlockSpec(memory_space=pltpu.HBM)
    vmem = pl.BlockSpec(memory_space=pltpu.VMEM)
    shapes = (
        jax.ShapeDtypeStruct((atoms, chan), F32),
        jax.ShapeDtypeStruct((3, atoms), F32),
        jax.ShapeDtypeStruct((EDGE, chan), F32),
        jax.ShapeDtypeStruct((levels, hidden), F32),
        jax.ShapeDtypeStruct((hidden, chan), F32),
    )
    results = pl.pallas_call(
        functools.partial(body, n_slab),
        out_shape=shapes,
        in_specs=[hbm] * 9,
        out_specs=(vmem,) * 5,
        scratch_shapes=scratch,
        compiler_params=pltpu.CompilerParams(
            collective_id=0, has_side_effects=True, vmem_limit_bytes=40 << 20
        ),
        name="ewald",
    )(
        *(
            pltpu.with_memory_space_constraint(v, pltpu.HBM)
            for v in (
                features,
                cotangent,
                positions,
                neighbours,
                counts.reshape(1, atoms),
                k_index,
                k_filter,
                w_radial,
                w_out,
            )
        )
    )
    return pl.pallas_call(
        store,
        out_shape=shapes,
        in_specs=[vmem] * 5,
        out_specs=(vmem,) * 5,
        compiler_params=pltpu.CompilerParams(vmem_limit_bytes=40 << 20),
        name="store",
    )(*results)


def solution(mesh):
    both = ("dom", "slab")
    in_specs = (P(both, None), P(both, None), P(None, both), P(None, both), P(both), P(), P(), P(), P())
    out_specs = (P(both, None), P(None, both), P(both, None), P(), P())
    return jax.shard_map(shards, mesh=mesh, in_specs=in_specs, out_specs=out_specs, check_vma=False)
```

```python
import functools
import math

import jax
import jax.numpy as jnp
from jax import lax
from jax.experimental import pallas as pl
from jax.experimental.pallas import tpu as pltpu
from jax.sharding import PartitionSpec as P

Z_HI, N_X, N_Y, N_CORE = 2, 4, 4, 2
EDGE = 8
PART = 8
BEFORE = 2
NEAR = 5
F32 = jnp.float32
BF16 = jnp.bfloat16

SIN_C = (3.1415926401307077, -5.167710083507896, 2.550077523214726, -0.5982912856213906, 0.07765766030763246)
COS_C = (
    0.9999999997799044,
    -4.934802137078806,
    4.058709159555702,
    -1.3352120030438075,
    0.23493731378604543,
    -0.024396324301093893,
)


def horner(coefs, u):
    y = coefs[-1] * u + coefs[-2]
    for k in coefs[-3::-1]:
        y = y * u + k
    return y


def turns(t):
    r = t - jnp.round(t)
    u = r * r
    s = r * horner(SIN_C, u)
    c = horner(COS_C, u)
    return 1.0 - 2.0 * (s * s), 2.0 * (s * c)


def split3(v):
    hi = v.astype(BF16)
    rest = v - hi.astype(F32)
    mid = rest.astype(BF16)
    lo = (rest - mid.astype(F32)).astype(BF16)
    return jnp.concatenate([hi.astype(F32), mid.astype(F32), lo.astype(F32), jnp.zeros_like(v)], axis=0).astype(BF16)


def nn(a, b):
    return lax.dot_general(a, b, (((1,), (0,)), ((), ())), preferred_element_type=F32)


def nt(a, b):
    return lax.dot_general(a, b, (((1,), (1,)), ((), ())), preferred_element_type=F32)


def body(
    n_slab,
    feat_hbm,
    cot_hbm,
    pos_hbm,
    nbr_hbm,
    cnt_hbm,
    kidx_hbm,
    kfil_hbm,
    wrad_hbm,
    wout_hbm,
    o_feat,
    o_pos,
    o_filter,
    o_radial,
    o_out,
    pos_ref,
    nbr_ref,
    cnt_ref,
    kidx_ref,
    wrad_ref,
    wout_ref,
    gfc,
    gpos,
    hfeat,
    hpos,
    csf,
    csh,
    ysend,
    yown,
    yrecv,
    zsend,
    zrecv,
    wbuf,
    kf8,
    picked,
    gfct,
    hot_s,
    act_s,
    dpre_s,
    rbf_s,
    chord_s,
    cosine_s,
    pacc,
    facc,
    xacc,
    outs_c,
    outr_c,
    outs_x,
    outr_x,
    kcol,
    krow,
    bufft,
    possp,
    cott,
    wradt,
    woutt,
    dbf,
    dbp,
    dgp,
    ownp,
    pwo,
    pwr,
    retf,
    retp,
    pw_a,
    pw_ar,
    pw_b,
    pw_br,
    pw_c,
    pw_cr,
    pw_d,
    loc_sem,
    g_s,
    g_r,
    gp_s,
    gp_r,
    h_s,
    h_r,
    hp_s,
    hp_r,
    y_s,
    y_r,
    z_s,
    z_r,
    za_s,
    za_r,
    ya_s,
    ya_r,
    oc_s,
    oc_r,
    ox_s,
    ox_r,
    rf_s,
    rf_r,
    rp_s,
    rp_r,
    pa_s,
    pa_r,
    pb_s,
    pb_r,
    pc_s,
    pc_r,
    pd_s,
    pd_r,
):
    atoms, chan = feat_hbm.shape
    slots = nbr_ref.shape[0]
    k_total = kidx_ref.shape[1]
    n_z = Z_HI * n_slab
    group = N_X * N_CORE
    k_loc = N_Y * n_z * EDGE
    n_dom = Z_HI * N_X * N_Y * N_CORE
    face = atoms // 8
    buf_rows = atoms + 4 * face
    nu = 1.0 / math.sqrt(atoms * n_dom * n_slab)
    mu = 1.0 / math.sqrt(k_total)

    dom = lax.axis_index("dom")
    slab = lax.axis_index("slab")
    core = lax.rem(dom, N_CORE)
    y = lax.rem(lax.div(dom, N_CORE), N_Y)
    x = lax.rem(lax.div(dom, N_CORE * N_Y), N_X)
    zh = lax.div(dom, N_CORE * N_Y * N_X)
    z = zh * n_slab + slab

    def dom_of(zh_, x_, y_, c_):
        return ((zh_ * N_X + x_) * N_Y + y_) * N_CORE + c_

    def at_xc(dx, dc):
        return (dom_of(zh, lax.rem(x + dx, N_X), y, lax.rem(core + dc, N_CORE)), slab)

    def at_y(d):
        return (dom_of(zh, x, lax.rem(y + d, N_Y), core), slab)

    def at_z(d):
        zz = lax.rem(z + d, n_z)
        return (dom_of(lax.div(zz, n_slab), x, y, core), lax.rem(zz, n_slab))

    at_dom = (
        (lax.rem(dom + n_dom - 1, n_dom), slab),
        (lax.rem(dom + 1, n_dom), slab),
        (dom, lax.rem(slab + n_slab - 1, n_slab)),
        (dom, lax.rem(slab + 1, n_slab)),
    )

    def copy(src, dst, ss, rs, dev):
        return pltpu.make_async_remote_copy(
            src_ref=src, dst_ref=dst, send_sem=ss, recv_sem=rs, device_id=dev, device_id_type=pl.DeviceIdType.MESH
        )

    xc = [(dx, dc) for dx in range(N_X) for dc in range(N_CORE)][1:]
    slot_of = {p: p[0] * N_CORE + p[1] for p in xc}
    far_first = sorted(xc, key=lambda p: -min(p[0], N_X - p[0]))
    near_first = far_first[::-1]

    peers = [at_xc(*p) for p in xc] + [at_y(d) for d in range(1, N_Y)] + [at_z(d) for d in range(1, n_z)]
    peers += [at_dom[0], at_dom[1]]
    barrier = pltpu.get_barrier_semaphore()
    for dev in peers:
        pl.semaphore_signal(barrier, inc=1, device_id=dev, device_id_type=pl.DeviceIdType.MESH)

    k_first = pl.multiple_of((dom * n_slab + slab) * EDGE, EDGE)
    loads = {}
    for i, (name, src, dst) in enumerate(
        (
            ("pos", pos_hbm, pos_ref),
            ("feat", feat_hbm, gfc.at[0, :, pl.ds(0, chan)]),
            ("cot", cot_hbm, gfc.at[0, :, pl.ds(chan, chan)]),
            ("kidx", kidx_hbm, kidx_ref),
            ("nbr", nbr_hbm, nbr_ref),
            ("cnt", cnt_hbm, cnt_ref),
            ("wrad", wrad_hbm, wrad_ref),
            ("wout", wout_hbm, wout_ref),
            ("filter", kfil_hbm.at[pl.ds(k_first, EDGE)], kf8),
        )
    ):
        loads[name] = pltpu.make_async_copy(src, dst, loc_sem.at[i])
        loads[name].start()
    m = lax.broadcasted_iota(jnp.int32, (k_loc, 1), 0)
    e = jnp.bitwise_and(m, EDGE - 1)
    place = lax.rem(lax.div(m, EDGE), n_z)
    bz = lax.rem(jnp.where(lax.rem(place, 2) == 1, lax.div(place + 1, 2), n_z - lax.div(place, 2)) + z, n_z)
    by = lax.rem(lax.div(m, EDGE * n_z) + y, N_Y)
    row = (dom_of(lax.div(bz, n_slab), x, by, core) * n_slab + lax.rem(bz, n_slab)) * EDGE + e
    column = lax.broadcasted_iota(jnp.int32, (k_loc, k_total), 1)
    picked[...] = jnp.where(row == column, 1.0, 0.0).astype(BF16)
    gpos[0] = jnp.zeros((8, atoms), F32)
    loads["pos"].wait()
    gpos[0, 0:3] = pos_ref[...]

    pl.semaphore_wait(barrier, len(peers))

    sent = []
    waits = {}

    def send(name, key, c):
        c.start()
        sent.append(c)
        waits[(name, key)] = c

    for p in far_first:
        s = slot_of[p]
        send("gp", s, copy(gpos.at[0], gpos.at[s], gp_s.at[s - 1], gp_r.at[s - 1], at_xc(*p)))
    loads["feat"].wait()
    loads["cot"].wait()
    x_order = sorted(range(1, N_X), key=lambda d: -min(d, N_X - d))
    for dx in x_order:
        s = dx * N_CORE
        send("g", s, copy(gfc.at[0], gfc.at[s], g_s.at[s - 1], g_r.at[s - 1], at_xc(dx, 0)))
    send("g", 1, copy(gfc.at[0], gfc.at[1], g_s.at[0], g_r.at[0], at_xc(0, 1)))
    for g in range(4):
        f = g ^ 1
        dev = at_dom[f]
        mine = gfc.at[0, pl.ds(f * face, face), pl.ds(0, chan)]
        send("h", g, copy(mine, hfeat.at[g], h_s.at[g], h_r.at[g], dev))
        send("hp", g, copy(gpos.at[0], hpos.at[g], hp_s.at[g], hp_r.at[g], dev))
    loads["kidx"].wait()

    pick = picked[...]
    k8 = jnp.concatenate([kidx_ref[...].astype(F32), jnp.zeros((5, k_total), F32)], axis=0)
    half = n_z * EDGE
    for d in range(N_Y):
        block = pick[d * half : (d + 1) * half]
        krow[d] = nt(k8.astype(BF16), jnp.concatenate([block, block], axis=0)).astype(BF16)
    kcol[...] = nt(pick, jnp.concatenate([k8, k8, k8, jnp.zeros_like(k8)], axis=0).astype(BF16)).astype(BF16)

    def tables(s):
        t = nn(kcol[...], split3(gpos[s]))
        cosine, sine = turns(t)
        lanes = slice(s * atoms, (s + 1) * atoms)
        both = jnp.stack([cosine.reshape(-1, EDGE, atoms), sine.reshape(-1, EDGE, atoms)], axis=1)
        csf[:, :, lanes] = both.reshape(-1, EDGE, atoms)
        csh[:, lanes] = both.reshape(-1, atoms).astype(BF16)

    tables(0)
    for p in near_first:
        s = slot_of[p]
        waits[("gp", s)].wait_recv()
        tables(s)

    def pair_setup():
        for g in range(4):
            waits[("h", g)].wait_recv()
            waits[("hp", g)].wait_recv()
        for name in ("nbr", "cnt", "wrad", "wout"):
            loads[name].wait()
        own_t = jnp.transpose(gfc[0, :, 0:chan].astype(F32))
        ghost = jnp.concatenate([hfeat[...].reshape(4 * face, chan), jnp.zeros((atoms - 4 * face, chan), BF16)], axis=0)
        ghost_t = jnp.transpose(ghost.astype(F32))
        bufft[...] = jnp.concatenate([own_t, ghost_t], axis=1).astype(BF16)
        cott[...] = jnp.transpose(gfc[0, :, chan : 2 * chan].astype(F32))
        wradt[...] = jnp.transpose(
            jnp.concatenate([wrad_ref[...].astype(F32), jnp.zeros((128 - wrad_ref.shape[0], 128), F32)], axis=0)
        ).astype(BF16)
        woutt[...] = jnp.transpose(wout_ref[...].astype(F32)).astype(BF16)
        lane = lax.broadcasted_iota(jnp.int32, (8, atoms), 1)
        ghost_pos = jnp.zeros((8, atoms), F32)
        for g in range(4):
            moved = pltpu.roll(hpos[g], (face if g % 2 else atoms - face), axis=1)
            ghost_pos = jnp.where((lane >= g * face) & (lane < (g + 1) * face), moved, ghost_pos)
        possp[:, 0:atoms] = split3(gpos[0])
        possp[:, atoms : 2 * atoms] = split3(ghost_pos)
        for ref in (dbf, dbp, ownp, pwo, pwr):
            ref[...] = jnp.zeros(ref.shape, F32)

    levels = wrad_ref.shape[0]
    rates = 0.5 * jnp.exp(
        lax.broadcasted_iota(jnp.int32, (levels, 1), 0).astype(F32) * (math.log(16.0) / (levels - 1))
    )

    span = 2
    width = span * atoms

    def weights(first):
        return jnp.concatenate(
            [cott[...] * jnp.where(cnt_ref[...] > first + j, slots**-0.5, 0.0) for j in range(span)], axis=1
        )

    def pair_first(q):
        first = q * span
        here = slice(q * width, (q + 1) * width)
        idx = jnp.concatenate([nbr_ref[first + j : first + j + 1, :] for j in range(span)], axis=1)
        hot = jnp.where(lax.broadcasted_iota(jnp.int32, (buf_rows, width), 0) == idx, 1.0, 0.0).astype(BF16)
        tp = nn(possp[:, 0:buf_rows], hot)
        target = tp[0:8] + tp[8:16] + tp[16:24]
        source = jnp.concatenate([gpos[0]] * span, axis=1)
        cosine, chord = turns(target - source)
        dist2 = jnp.sum(chord * chord, axis=0, keepdims=True)
        rbf = jnp.exp(-rates * dist2)
        rbf_h = rbf.astype(BF16)
        pre = nn(wradt[:, 0:levels], rbf_h)
        gate = 0.5 * jnp.tanh(0.5 * pre) + 0.5
        act = (pre * gate).astype(BF16)
        dphi = (weights(first) * nn(bufft[:, 0:buf_rows], hot)).astype(BF16)
        pwo[...] += nt(act, dphi)
        d_act = nn(wout_ref[...], dphi)
        dpre = (d_act * gate * (1.0 + pre * (1.0 - gate))).astype(BF16)
        pwr[...] += nt(rbf_h, dpre)
        hot_s[:, here] = hot
        act_s[:, here] = act
        dpre_s[:, here] = dpre
        rbf_s[:, here] = rbf
        chord_s[:, here] = chord
        cosine_s[:, here] = cosine

    def pair_second(q):
        here = slice(q * width, (q + 1) * width)
        hot = hot_s[:, here]
        given = weights(q * span) * nn(woutt[...], act_s[:, here])
        given_hi = given.astype(BF16)
        given_lo = (given - given_hi.astype(F32)).astype(BF16)
        added = nt(hot, jnp.concatenate([given_hi, given_lo], axis=0))
        dbf[...] += added[:, 0:chan] + added[:, chan : 2 * chan]
        d_rbf = nn(wrad_ref[...], dpre_s[:, here])
        d_chord2 = -jnp.sum(d_rbf * rates * rbf_s[:, here], axis=0, keepdims=True)
        dmove = (2.0 * mu) * d_chord2 * chord_s[:, here] * cosine_s[:, here]
        move_hi = dmove.astype(BF16).astype(F32)
        moves = nt(jnp.concatenate([move_hi, dmove - move_hi], axis=0).astype(BF16), hot)
        dbp[...] += moves[0:8] + moves[8:16]
        for j in range(span):
            ownp[...] -= dmove[:, j * atoms : (j + 1) * atoms]

    out_rows = pwo.shape[0] // group
    rad_rows = levels // group
    my_piece = x * N_CORE + core

    def pair_sends():
        for j in range(group):
            pw_a[j, 0:out_rows] = pwo[j * out_rows : (j + 1) * out_rows, :]
            tail = pwr[j * rad_rows : (j + 1) * rad_rows, :]
            pw_a[j, out_rows:] = jnp.concatenate([tail, jnp.zeros((8 - rad_rows, tail.shape[1]), F32)], axis=0)
        for p in far_first:
            s = slot_of[p]
            piece = lax.rem(x + p[0], N_X) * N_CORE + lax.rem(core + p[1], N_CORE)
            send("pa", s, copy(pw_a.at[piece], pw_ar.at[s - 1], pa_s.at[s - 1], pa_r.at[s - 1], at_xc(*p)))

    def hand_over(dx):
        s = dx * N_CORE
        waits[("g", s)].wait_recv()
        send("g", s + 1, copy(gfc.at[s], gfc.at[s + 1], g_s.at[s], g_r.at[s], at_xc(0, 1)))

    def chip_part(dx, rows):
        lanes = slice(dx * N_CORE * atoms, (dx + 1) * N_CORE * atoms)
        return nn(csh[rows, lanes], gfc[dx * N_CORE : (dx + 1) * N_CORE].reshape(N_CORE * atoms, 2 * chan))

    dz_at = [(p + 1) // 2 if p % 2 else (n_z - p // 2) % n_z for p in range(n_z)]
    place_of = {dz: p for p, dz in enumerate(dz_at)}
    z_rows = 2 * EDGE
    near_z = n_z * NEAR // 8
    parts = ((near_z, n_z), (0, near_z))
    y_rows = n_z * 2 * EDGE
    near_x = x_order[::-1]
    all_rows = slice(0, 2 * k_loc)
    chunks = slots // 2
    for dx in near_x[:-1]:
        hand_over(dx)
    waits[("g", 1)].wait_recv()
    pacc[...] = chip_part(0, all_rows)
    hand_over(near_x[-1])
    for dx in near_x[:-1]:
        waits[("g", dx * N_CORE + 1)].wait_recv()
        pacc[...] += chip_part(dx, all_rows)
    waits[("g", near_x[-1] * N_CORE + 1)].wait_recv()
    y_order = sorted(range(1, N_Y), key=lambda d: -min(d, N_Y - d))

    def send_y(g, d):
        rows = pl.ds(parts[g][0] * z_rows, (parts[g][1] - parts[g][0]) * z_rows)
        i = 2 * d - 2 + g
        send("y", (g, d), copy(ysend.at[d - 1, rows], yrecv.at[d - 1, rows], y_s.at[i], y_r.at[i], at_y(d)))

    for d in y_order + [0]:
        rows = slice(d * y_rows, (d + 1) * y_rows)
        part = pacc[rows, :] + chip_part(near_x[-1], rows)
        if d:
            ysend[d - 1] = part.astype(BF16)
            send_y(0, d)
        else:
            yown[...] = part
    for d in y_order:
        send_y(1, d)

    first_part = chunks * PART // 8
    pair_setup()
    for q in range(first_part):
        pair_first(q)
    if first_part == chunks:
        pair_sends()

    for g, (lo, hi) in enumerate(parts):
        rows = slice(lo * z_rows, hi * z_rows)
        total = yown[rows, :]
        for d in range(1, N_Y):
            waits[("y", (g, d))].wait_recv()
            total = total + yrecv[d - 1, rows].astype(F32)
        for p in range(hi - 1, lo - 1, -1):
            block = total[(p - lo) * z_rows : (p - lo + 1) * z_rows, :]
            d = dz_at[p]
            if d:
                zsend[d - 1] = block.astype(BF16)
                send("z", d, copy(zsend.at[d - 1], zrecv.at[d - 1], z_s.at[d - 1], z_r.at[d - 1], at_z(d)))
            else:
                mine = block
    for q in range(first_part, chunks):
        pair_first(q)
    if first_part < chunks:
        pair_sends()

    for s in range(group):
        gfct[:, s * atoms : (s + 1) * atoms] = jnp.transpose(gfc[s].astype(F32)).astype(BF16)

    for d in range(1, n_z):
        waits[("z", d)].wait_recv()
        mine = mine + zrecv[d - 1].astype(F32)
    mine = nu * mine
    loads["filter"].wait()
    kf = jnp.concatenate([kf8[...], kf8[...]], axis=0)
    wbuf[0, 0] = jnp.concatenate([kf * mine[:, chan : 2 * chan], kf * mine[:, 0:chan]], axis=1).astype(BF16)
    z_order = dz_at[:0:-1]
    for d in z_order:
        there = n_z - d
        to = wbuf.at[0, place_of[there]]
        send("za", there, copy(wbuf.at[0, 0], to, za_s.at[d - 1], za_r.at[there - 1], at_z(d)))
    o_filter[...] = (
        mine[0:EDGE, 0:chan] * mine[0:EDGE, chan : 2 * chan]
        + mine[EDGE : 2 * EDGE, 0:chan] * mine[EDGE : 2 * EDGE, chan : 2 * chan]
    )

    before = chunks * BEFORE // 8
    for q in range(before):
        pair_second(q)
    for p in xc:
        waits[("pa", slot_of[p])].wait_recv()
    piece_sum = pw_a[my_piece]
    for s in range(group - 1):
        piece_sum = piece_sum + pw_ar[s]
    pw_b[...] = piece_sum
    for d in z_order:
        send("pb", d, copy(pw_b, pw_br.at[d - 1], pb_s.at[d - 1], pb_r.at[d - 1], at_z(d)))
    for q in range(before, chunks):
        pair_second(q)
    dgp[...] = jnp.concatenate([dbp[:, atoms:buf_rows], jnp.zeros((8, 2 * atoms - buf_rows), F32)], axis=1)
    for g in range(4):
        send("rf", g, copy(dbf.at[pl.ds(atoms + g * face, face)], retf.at[g], rf_s.at[g], rf_r.at[g], at_dom[g]))
        send("rp", g, copy(dgp, retp.at[g], rp_s.at[g], rp_r.at[g], at_dom[g]))

    for g in (1, 0):
        lo, hi = parts[g]
        for p in range(max(lo, 1), hi):
            waits[("za", dz_at[p])].wait_recv()
        for d in y_order:
            there = N_Y - d
            i = 2 * there - 2 + g
            blocks = pl.ds(lo, hi - lo)
            to = wbuf.at[there, blocks]
            send("ya", (g, there), copy(wbuf.at[0, blocks], to, ya_s.at[2 * d - 2 + g], ya_r.at[i], at_y(d)))

    for d in range(1, n_z):
        waits[("pb", d)].wait_recv()
        piece_sum = piece_sum + pw_br[d - 1]
    pw_c[...] = piece_sum
    for d in y_order:
        send("pc", d, copy(pw_c, pw_cr.at[d - 1], pc_s.at[d - 1], pc_r.at[d - 1], at_y(d)))

    def turned(d):
        return jnp.transpose(wbuf[d].reshape(y_rows, 2 * chan)[:, 0:chan].astype(F32)).astype(BF16)

    def give_back(d, fg_t, first, count):
        lanes = slice(first * atoms, (first + count) * atoms)
        rows = slice(d * y_rows, (d + 1) * y_rows)
        w = wbuf[d].reshape(y_rows, 2 * chan)
        d_feat_t = nn(fg_t, csh[rows, lanes])
        pq = nn(w, gfct[:, lanes]).reshape(-1, 2, EDGE, count * atoms)
        cs = csf[d * y_rows // EDGE : (d + 1) * y_rows // EDGE, :, lanes].reshape(-1, 2, EDGE, count * atoms)
        wave = (cs[:, 0] * pq[:, 1] - cs[:, 1] * pq[:, 0]).reshape(half, count * atoms)
        hi = wave.astype(BF16).astype(F32)
        d_pos = mu * nn(krow[d], jnp.concatenate([hi, wave - hi], axis=0).astype(BF16))
        return d_feat_t, d_pos

    for d in [0] + y_order[::-1][:-1]:
        if d:
            waits[("ya", (1, d))].wait_recv()
            waits[("ya", (0, d))].wait_recv()
        fg_t = turned(d)
        for first in range(0, group, 2):
            lanes = slice(first * atoms, (first + 2) * atoms)
            d_feat_t, d_pos = give_back(d, fg_t, first, 2)
            if d:
                facc[:, lanes] += d_feat_t
                xacc[:, lanes] += d_pos
            else:
                facc[:, lanes] = d_feat_t
                xacc[:, lanes] = d_pos
    for d in range(1, N_Y):
        waits[("pc", d)].wait_recv()
        piece_sum = piece_sum + pw_cr[d - 1]
    pw_d[my_piece] = nu * piece_sum
    for p in far_first:
        s = slot_of[p]
        send("pd", s, copy(pw_d.at[my_piece], pw_d.at[my_piece], pd_s.at[s - 1], pd_r.at[s - 1], at_xc(*p)))
    for g in range(4):
        waits[("rf", g)].wait_recv()
        waits[("rp", g)].wait_recv()
    lane = lax.broadcasted_iota(jnp.int32, (8, atoms), 1)
    short_pos = dbp[:, 0:atoms] + ownp[...]
    for g in range(4):
        f = g ^ 1
        moved = pltpu.roll(retp[g], (atoms - face if g % 2 else face), axis=1)
        short_pos = short_pos + jnp.where((lane >= f * face) & (lane < (f + 1) * face), moved, 0.0)
        rows = slice(f * face, (f + 1) * face)
        dbf[rows, :] += retf[g]
    ownp[...] = short_pos
    last = y_order[0]
    waits[("ya", (1, last))].wait_recv()
    waits[("ya", (0, last))].wait_recv()
    fg_last = turned(last)

    def whole(s):
        lanes = slice(s * atoms, (s + 1) * atoms)
        d_feat_t, d_pos = give_back(last, fg_last, s, 1)
        return facc[:, lanes] + d_feat_t, xacc[:, lanes] + d_pos

    for dx in x_order + [0]:
        d_feat_t, d_pos = whole(dx * N_CORE + 1)
        outs_c[dx, 0:chan] = d_feat_t
        outs_c[dx, chan:] = d_pos
        send("oc", dx, copy(outs_c.at[dx], outr_c.at[dx], oc_s.at[dx], oc_r.at[dx], at_xc(0, 1)))
    for dx in x_order:
        d_feat_t, d_pos = whole(dx * N_CORE)
        waits[("oc", dx)].wait_recv()
        d_feat_t = d_feat_t + outr_c[dx, 0:chan]
        d_pos = d_pos + outr_c[dx, chan:]
        pos_hi = d_pos.astype(BF16).astype(F32)
        outs_x[dx - 1] = jnp.concatenate([d_feat_t, pos_hi, d_pos - pos_hi], axis=0).astype(BF16)
        send("ox", dx, copy(outs_x.at[dx - 1], outr_x.at[dx - 1], ox_s.at[dx - 1], ox_r.at[dx - 1], at_xc(N_X - dx, 0)))

    long_t, long_pos = whole(0)
    waits[("oc", 0)].wait_recv()
    long_t = long_t + outr_c[0, 0:chan]
    long_pos = long_pos + outr_c[0, chan:]
    late = [waits[("ox", dx)] for dx in x_order]
    for c in sent:
        if all(c is not other for other in late):
            c.wait_send()
    for p in xc:
        waits[("pd", slot_of[p])].wait_recv()
    for j in range(group):
        o_out[j * out_rows : (j + 1) * out_rows, :] = pw_d[j, 0:out_rows]
        o_radial[j * rad_rows : (j + 1) * rad_rows, :] = pw_d[j, out_rows : out_rows + rad_rows]
    for dx in near_x:
        waits[("ox", dx)].wait_recv()
        got = outr_x[dx - 1].astype(F32)
        long_t = long_t + got[0:chan]
        long_pos = long_pos + got[chan : chan + 8] + got[chan + 8 : chan + 16]
    o_feat[...] = jnp.transpose(long_t) + dbf[0:atoms, :]
    o_pos[...] = (long_pos + ownp[...])[0:3]
    for c in late:
        c.wait_send()


def store(*refs):
    n = len(refs) // 2
    for src, dst in zip(refs[:n], refs[n:]):
        dst[...] = src[...]


def shards(features, cotangent, positions, neighbours, counts, k_index, k_filter, w_radial, w_out):
    n_slab = lax.axis_size("slab")
    atoms, chan = features.shape
    levels, hidden = w_radial.shape
    group = N_X * N_CORE
    n_z = Z_HI * n_slab
    k_loc = N_Y * n_z * EDGE
    face = atoms // 8
    buf_rows = atoms + 4 * face
    piece = hidden // group + 8
    pairs = atoms * neighbours.shape[0]
    v = pltpu.VMEM
    dma = pltpu.SemaphoreType.DMA
    scratch = [
        v(positions.shape, F32),
        v(neighbours.shape, jnp.int32),
        v((1, atoms), jnp.int32),
        v(k_index.shape, jnp.int32),
        v(w_radial.shape, BF16),
        v(w_out.shape, BF16),
        v((group, atoms, 2 * chan), BF16),
        v((group, 8, atoms), F32),
        v((4, face, chan), BF16),
        v((4, 8, atoms), F32),
        v((2 * k_loc // EDGE, EDGE, group * atoms), F32),
        v((2 * k_loc, group * atoms), BF16),
        v((N_Y - 1, 2 * n_z * EDGE, 2 * chan), BF16),
        v((2 * n_z * EDGE, 2 * chan), F32),
        v((N_Y - 1, 2 * n_z * EDGE, 2 * chan), BF16),
        v((n_z - 1, 2 * EDGE, 2 * chan), BF16),
        v((n_z - 1, 2 * EDGE, 2 * chan), BF16),
        v((N_Y, n_z, 2 * EDGE, 2 * chan), BF16),
        v((EDGE, chan), F32),
        v((k_loc, k_index.shape[1]), BF16),
        v((2 * chan, group * atoms), BF16),
        v((buf_rows, pairs), BF16),
        v((hidden, pairs), BF16),
        v((hidden, pairs), BF16),
        v((levels, pairs), F32),
        v((8, pairs), F32),
        v((8, pairs), F32),
        v((2 * k_loc, 2 * chan), F32),
        v((chan, group * atoms), F32),
        v((8, group * atoms), F32),
        v((N_X, chan + 8, atoms), F32),
        v((N_X, chan + 8, atoms), F32),
        v((N_X - 1, chan + 16, atoms), BF16),
        v((N_X - 1, chan + 16, atoms), BF16),
        v((k_loc, 32), BF16),
        v((N_Y, 8, 2 * n_z * EDGE), BF16),
        v((chan, 2 * atoms), BF16),
        v((32, 2 * atoms), BF16),
        v((chan, atoms), F32),
        v((hidden, 128), BF16),
        v((chan, hidden), BF16),
        v((buf_rows, chan), F32),
        v((8, buf_rows), F32),
        v((8, atoms), F32),
        v((8, atoms), F32),
        v((hidden, chan), F32),
        v((levels, hidden), F32),
        v((4, face, chan), F32),
        v((4, 8, atoms), F32),
        v((group, piece, chan), F32),
        v((group - 1, piece, chan), F32),
        v((piece, chan), F32),
        v((n_z - 1, piece, chan), F32),
        v((piece, chan), F32),
        v((N_Y - 1, piece, chan), F32),
        v((group, piece, chan), F32),
        dma((9,)),
    ]
    for n in (group - 1, group - 1, 4, 4, 2 * N_Y - 2, n_z - 1, n_z - 1, 2 * N_Y - 2):
        scratch += [dma((n,)), dma((n,))]
    for n in (N_X, N_X - 1, 4, 4, group - 1, n_z - 1, N_Y - 1, group - 1):
        scratch += [dma((n,)), dma((n,))]
    hbm = pl.BlockSpec(memory_space=pltpu.HBM)
    vmem = pl.BlockSpec(memory_space=pltpu.VMEM)
    shapes = (
        jax.ShapeDtypeStruct((atoms, chan), F32),
        jax.ShapeDtypeStruct((3, atoms), F32),
        jax.ShapeDtypeStruct((EDGE, chan), F32),
        jax.ShapeDtypeStruct((levels, hidden), F32),
        jax.ShapeDtypeStruct((hidden, chan), F32),
    )
    results = pl.pallas_call(
        functools.partial(body, n_slab),
        out_shape=shapes,
        in_specs=[hbm] * 9,
        out_specs=(vmem,) * 5,
        scratch_shapes=scratch,
        compiler_params=pltpu.CompilerParams(
            collective_id=0, has_side_effects=True, vmem_limit_bytes=40 << 20
        ),
        name="ewald",
    )(
        *(
            pltpu.with_memory_space_constraint(v, pltpu.HBM)
            for v in (
                features,
                cotangent,
                positions,
                neighbours,
                counts.reshape(1, atoms),
                k_index,
                k_filter,
                w_radial,
                w_out,
            )
        )
    )
    return pl.pallas_call(
        store,
        out_shape=shapes,
        in_specs=[vmem] * 5,
        out_specs=(vmem,) * 5,
        compiler_params=pltpu.CompilerParams(vmem_limit_bytes=40 << 20),
        name="store",
    )(*results)


def solution(mesh):
    both = ("dom", "slab")
    in_specs = (P(both, None), P(both, None), P(None, both), P(None, both), P(both), P(), P(), P(), P())
    out_specs = (P(both, None), P(None, both), P(both, None), P(), P())
    return jax.shard_map(shards, mesh=mesh, in_specs=in_specs, out_specs=out_specs, check_vma=False)
```
